512 devices in a mesh: ep: 64 (over z, y), os: 8 (over x, core).
Axes of the slice: x: 4, y: 4, z: 16, core: 2. Of those that a mesh axis runs over, the one named last changes fastest.
Arguments:
- tokens: bfloat16 [8192, 2048], P('ep', 'os'), may hold values from -6 to 6
- cotangent: bfloat16 [8192, 2048], P('ep', 'os'), may hold values from -6 to 6
- expert_ids: int32 [8192, 8], P('ep'), may hold values from 0 to 63, all different within a row; in each aligned block of 128 rows (0 to 127, 128 to 255, ...) at most 24 rows name the same one
- route_weight: float32 [8192, 8], P('ep'), may hold values from 0.1 to 1
- placement: int32 [64], replicated, may hold values from 0 to 63, each once
- swap_flags: int32 [2, 64], replicated, may hold values from 0 to 1, as said below
- params: bfloat16 [64, 3, 2048, 384], P('ep', None, 'os'), may hold values from -1 to 1
- first_moment: bfloat16 [64, 3, 2048, 384], P('ep', None, 'os'), may hold values from -6 to 6
- second_moment: bfloat16 [64, 3, 2048, 384], P('ep', None, 'os'), may hold values from 0.5 to 20
Outputs:
- mixed: bfloat16 [8192, 2048], P('ep', 'os')
- input_grad: bfloat16 [8192, 2048], P('ep', 'os')
- new_params: bfloat16 [64, 3, 2048, 384], P('ep', None, 'os')
- new_first: bfloat16 [64, 3, 2048, 384], P('ep', None, 'os')
- new_second: bfloat16 [64, 3, 2048, 384], P('ep', None, 'os')
The draws below stay inside these ranges and needn't reach their ends.
Inputs may be any that keep to these rules, and one draw needn't show every extreme that they name: `expert_ids`: each row names 8 different experts; in each aligned block of 128 rows (the rows of one index of ep) no expert is named by more than 24 rows, a bound that some block reaches. `placement`: A permutation of the 64 expert ids. swap_flags[r, i] = swap_flags[r, i XOR 2^b_r] with b_0 = log2(64) - 1 and b_1 = 0.
All inputs are finite; a program needn't handle non-finite values.
Results may differ from the reference program's by a relative error of at most 0.023.
Values may be sent and summed in bfloat16 or wider, within the bound.
A program may use at most 64 MiB of HBM per device.

```python
import math
import jax
import jax.numpy as jnp
import numpy as np
from jax import lax

D = 2048
TOP = 8
HW = 384
TOK_DEV = 128
EXPERTS = 64
TOKENS = 8192
CAP = 24
N_EP = 64
N_OS = 8


def draw_swap_flags(key, part):
    index = jnp.arange(EXPERTS, dtype=jnp.int32)
    bits = [EXPERTS.bit_length() - 2, 0]
    rounds = []
    for rnd in range(2):
        coins = jax.random.randint(jax.random.fold_in(key, rnd + 11), (EXPERTS,), 0, 2, dtype=jnp.int32)
        lowend = EXPERTS - 1 - (1 << bits[rnd])
        coins = coins.at[0].set(1).at[lowend].set(1)
        lower = index - (index & 1 << bits[rnd])
        rounds.append(coins[lower])
    return jnp.stack(rounds).astype(jnp.int32)


def draw_params(key, part):
    shape = (EXPERTS, 3, D, HW)
    base = jnp.clip(jax.random.normal(key, shape, jnp.float32), -6.0, 6.0)
    factor = jnp.where(jnp.arange(3) < 2, D ** (-0.5), HW ** (-0.5)).astype(jnp.float32).reshape(1, 3, 1, 1)
    return (base * factor).astype(jnp.bfloat16)


def block_levels(stream_key, dims, cuts, smallest, high):
    def one(dim, shards_of):
        steps = jax.random.uniform(jax.random.fold_in(jax.random.fold_in(stream_key, 6), dim), (shards_of,), jnp.float32, smallest / len(cuts), high / len(cuts))
        return jnp.repeat(jnp.exp(steps), dims[dim] // shards_of).reshape((-1,) + (1,) * (len(dims) - dim - 1))

    level = one(*cuts[0])
    for cut in cuts[1:]:
        level = level * one(*cut)
    return level


def shared_out(rng, own, number, rows, count, top, limit, lean):
    order = jax.random.permutation(rng, count)
    crowded, common = portions_of(count, rows * top, limit, lean, True), portions_of(count, rows * top, limit, lean, False)
    places = jnp.arange(count)

    def named(tallies, rotation):
        used = int((tallies > 0).sum())
        fixed = max(1, used // 4)
        shifted = fixed + (places - fixed + rotation * (used - fixed)) % max(1, count - fixed)
        return jnp.zeros((count,), jnp.int32).at[order[jnp.where(places < fixed, places, shifted)]].set(jnp.asarray(tallies, jnp.int32))

    tallies = jnp.where(number % 4 == 0, named(crowded, number // 4), named(common, number - number // 4 - 1))
    mixed = jax.random.permutation(jax.random.fold_in(own, 3), count)
    donor, taker = mixed[0:count // 2 * 2:2], mixed[1:count // 2 * 2:2]
    slack = jnp.minimum(tallies[donor] - 1, limit - tallies[taker]) // 2
    slack = jnp.where((donor == order[0]) | (taker == order[0]) | (tallies[taker] == 0), 0, jnp.maximum(slack, 0))
    shifted = jax.random.randint(jax.random.fold_in(own, 4), (count // 2,), 0, 1 << 20) % (slack + 1)
    tallies = tallies.at[donor].add(-shifted).at[taker].add(shifted)
    items = jnp.searchsorted(jnp.cumsum(tallies), jnp.arange(rows * top), side="right").astype(jnp.int32)
    listing = items.reshape(top, rows).T
    listing = listing[jax.random.permutation(jax.random.fold_in(own, 1), rows)]
    rotation = jax.random.randint(jax.random.fold_in(own, 2), (rows, 1), 0, top)
    return jnp.take_along_axis(listing, (jnp.arange(top)[None, :] + rotation) % top, axis=1)


def portions_of(count, total, most, skew, full):
    loads = [(1 << 20) // math.isqrt(standing ** skew) + 1 for standing in range(1, count + 1)]
    largest = most if full else min(most, max(-(-total // count), total * loads[0] // sum(loads)))
    least = 1 if total - largest >= count - 1 else 0
    holding, spare = [largest] + [least] * (count - 1), total - largest - least * (count - 1)
    while spare > 0:
        candidates = [i for i in range(1, count) if holding[i] < largest] or [i for i in range(1, count) if holding[i] < most]
        whole, budget = sum([loads[i] for i in candidates]), spare
        for i in candidates:
            extra = min(most - holding[i], max(1, budget * loads[i] // whole), spare)
            holding[i] = holding[i] + extra
            spare = spare - extra
    return np.array(holding)


def centred(stream_key, extent, deviation, reach, split=(), kind=jnp.bfloat16):
    result = deviation * jax.random.normal(stream_key, extent, jnp.float32)
    if split:
        result = result * block_levels(stream_key, extent, split, -0.22, 0.18)
    return jnp.clip(result, -reach, reach).astype(kind)


def setup_inputs(seed: int = 0) -> dict:
    key_of = jax.random.split(jax.random.key(seed), 10)
    tokens = centred(key_of[0], (TOKENS, D), 1.0, 6.0, ((0, 64), (1, 8)))
    cotangent = centred(key_of[1], (TOKENS, D), 1.0, 6.0, ((0, 64), (1, 8)))
    expert_ids_keys = jax.random.split(jax.random.fold_in(key_of[2], 1), TOKENS // TOK_DEV)
    expert_ids_turns = jax.random.permutation(jax.random.fold_in(key_of[2], 3), TOKENS // TOK_DEV)
    expert_ids = jax.vmap(lambda own, number: shared_out(jax.random.fold_in(key_of[2], 2), own, number, TOK_DEV, EXPERTS, TOP, CAP, 2))(expert_ids_keys, expert_ids_turns).reshape((TOKENS, TOP))
    route_weight = jnp.clip(jnp.exp(math.log(1.0) - 2.3025851 * jax.random.uniform(key_of[3], (TOKENS, TOP), jnp.float32) ** block_levels(key_of[3], (TOKENS, TOP), ((0, 64),), -0.2, 0.2)), 0.1, 1.0)
    placement = jax.random.permutation(key_of[4], EXPERTS).astype(jnp.int32)
    swap_flags = draw_swap_flags(jax.random.fold_in(key_of[9], 71), 0)
    params = draw_params(jax.random.fold_in(key_of[9], 71), 0)
    first_moment = centred(key_of[7], (EXPERTS, 3, D, HW), 1.0, 6.0, ((0, 64), (2, 8)))
    second_moment = jnp.clip(jnp.exp(math.log(20.0) - 3.6888795 * jax.random.uniform(key_of[8], (EXPERTS, 3, D, HW), jnp.float32) ** block_levels(key_of[8], (EXPERTS, 3, D, HW), ((0, 64), (2, 8)), -0.2, 0.2)), 0.5, 20.0).astype(jnp.bfloat16)
    return dict(tokens=tokens, cotangent=cotangent, expert_ids=expert_ids, route_weight=route_weight, placement=placement, swap_flags=swap_flags, params=params, first_moment=first_moment, second_moment=second_moment)


beta_first = 0.9
beta_second = 0.999
learn_rate = 0.01
adam_eps = 1e-08
adam_count = 10.0

def adam_update(weight, first, second, grad):
    first_new = beta_first * first.astype(jnp.float32) + (1.0 - beta_first) * grad
    second_new = beta_second * second.astype(jnp.float32) + (1.0 - beta_second) * grad * grad
    first_hat = first_new / (1.0 - beta_first ** adam_count)
    second_hat = second_new / (1.0 - beta_second ** adam_count)
    weight_new = weight.astype(jnp.float32) - learn_rate * first_hat / (jnp.sqrt(second_hat) + adam_eps)
    return (weight_new.astype(jnp.bfloat16), first_new.astype(jnp.bfloat16), second_new.astype(jnp.bfloat16))

def partial_sum(parts):
    rounded = parts.astype(jnp.bfloat16)
    rounded = lax.optimization_barrier(rounded)
    return lax.optimization_barrier(jnp.sum(rounded.astype(jnp.float32), axis=0))

def expert_pass(x_rows, dy_rows, weight):
    shard = D // N_OS
    xs = x_rows.astype(jnp.float32).reshape(-1, N_OS, shard)
    dys = dy_rows.astype(jnp.float32).reshape(-1, N_OS, shard)
    wfull = weight.astype(jnp.float32)
    wparts = wfull.reshape(3, N_OS, shard, HW)
    both = partial_sum(jnp.einsum('ros,kosh->okrh', xs, wparts[:2]))
    gate = both[0]
    up = both[1]
    sigma = jax.nn.sigmoid(gate)
    active = gate * sigma
    hidden = (active * up).astype(jnp.bfloat16)
    hidden_f = hidden.astype(jnp.float32)
    rows_out = jnp.einsum('rh,dh->rd', hidden_f, wfull[2]).astype(jnp.bfloat16)
    back = partial_sum(jnp.einsum('ros,osh->orh', dys, wparts[2]))
    d_gate = (back * up * sigma * (1.0 + gate * (1.0 - sigma))).astype(jnp.bfloat16)
    d_up = (back * active).astype(jnp.bfloat16)
    deriv = jnp.stack((d_gate, d_up)).astype(jnp.float32)
    x_f = x_rows.astype(jnp.float32)
    grad_in = jnp.einsum('rd,krh->kdh', x_f, deriv)
    grad_out = jnp.einsum('rd,rh->dh', dy_rows.astype(jnp.float32), hidden_f)
    grad = jnp.concatenate((grad_in, grad_out[None]), axis=0)
    rows_grad = jnp.einsum('krh,kdh->rd', deriv, wfull[:2]).astype(jnp.bfloat16)
    return (rows_out, rows_grad, grad)

def reference(tokens, cotangent, expert_ids, route_weight, placement, swap_flags, params, first_moment, second_moment):
    index = jnp.arange(EXPERTS, dtype=jnp.int32)
    place = placement
    state = (params, first_moment, second_moment)
    bits = [EXPERTS.bit_length() - 2, 0]
    for rnd in range(2):
        partner = index ^ 1 << bits[rnd]
        chosen = swap_flags[rnd] == 1
        state = tuple((jnp.where(chosen[:, None, None, None], s[partner], s) for s in state))
        place = jnp.where(chosen, place[partner], place)
    held_params, held_first, held_second = state
    holder = jnp.zeros((EXPERTS,), jnp.int32).at[place].set(index)
    dest = holder[expert_ids].reshape(N_EP, TOK_DEV * TOP)
    onehot = (dest[:, :, None] == index[None, None, :]).astype(jnp.int32)
    before = jnp.cumsum(onehot, axis=1) - onehot
    slot = lax.optimization_barrier(jnp.sum(before * onehot, axis=2)).astype(jnp.int32)
    source = jnp.broadcast_to(jnp.arange(N_EP, dtype=jnp.int32)[:, None], dest.shape)
    flat_rows = jnp.arange(TOKENS * TOP, dtype=jnp.int32).reshape(N_EP, TOK_DEV * TOP)
    table = jnp.zeros((EXPERTS, N_EP, CAP), jnp.int32).at[dest, source, slot].set(flat_rows + 1)
    weights_flat = route_weight.reshape(-1)

    def one_expert(carry, inputs):
        mixed_acc, grad_acc = carry
        rows, weight, first, second = inputs
        rows = rows.reshape(-1)
        filled = rows > 0
        src = jnp.maximum(rows - 1, 0).astype(jnp.int32)
        owner = (src // TOP).astype(jnp.int32)
        x_rows = jnp.where(filled[:, None], tokens[owner], jnp.zeros((), jnp.bfloat16))
        dy_rows = jnp.where(filled[:, None], weights_flat[src][:, None] * cotangent[owner].astype(jnp.float32), jnp.float32(0.0)).astype(jnp.bfloat16)
        rows_out, rows_grad, grad = expert_pass(x_rows, dy_rows, weight)
        scale = jnp.where(filled, weights_flat[src], jnp.float32(0.0))
        mixed_acc = mixed_acc.at[owner].add(scale[:, None] * rows_out.astype(jnp.float32))
        grad_acc = grad_acc.at[owner].add(jnp.where(filled[:, None], rows_grad.astype(jnp.float32), jnp.float32(0.0)))
        return ((mixed_acc, grad_acc), adam_update(weight, first, second, grad))
    init = (jnp.zeros((TOKENS, D), jnp.float32), jnp.zeros((TOKENS, D), jnp.float32))
    (mixed_acc, grad_acc), updated = lax.scan(one_expert, init, (table, held_params, held_first, held_second))
    new_params, new_first, new_second = updated
    return (mixed_acc.astype(jnp.bfloat16), grad_acc.astype(jnp.bfloat16), new_params, new_first, new_second)
```

```python
import functools

import jax
import jax.numpy as jnp
from jax import lax
from jax.experimental import pallas as pl
from jax.experimental.pallas import tpu as pltpu
from jax.sharding import PartitionSpec as P

MESH = pl.DeviceIdType.MESH
F32 = jnp.float32
BF16 = jnp.bfloat16

beta_first = 0.9
beta_second = 0.999
learn_rate = 0.01
adam_eps = 1e-08
adam_count = 10.0

NY = 4
NC = 2


def dot(a, b):
    return jnp.dot(a, b, preferred_element_type=F32)


def dot_nt(a, b):
    return lax.dot_general(a, b, (((1,), (1,)), ((), ())), preferred_element_type=F32)


def dot_tn(a, b):
    return lax.dot_general(a, b, (((0,), (0,)), ((), ())), preferred_element_type=F32)


def kernel(
    nz,
    nx,
    cap,
    place,
    flags,
    ids,
    rw,
    tok,
    cot,
    par,
    mom1,
    mom2,
    mixed,
    igrad,
    new_p,
    new_m,
    new_v,
    tc,
    mt,
    yb,
    zs,
    zr,
    wf,
    sx,
    rx,
    p01,
    phi,
    plo,
    psnd,
    own,
    crecv,
    xs,
    xr,
    hh,
    yo,
    yr,
    prt,
    rss,
    rsr,
    gr,
    s_loc,
    s_ag,
    s_y,
    s_z,
    s_yx,
    s_c,
    s_x,
    s_h,
    s_hc,
    s_yo,
    s_rs,
):
    ep = lax.axis_index("ep")
    osi = lax.axis_index("os")
    z, y = lax.div(ep, NY), lax.rem(ep, NY)
    x, c = lax.div(osi, NC), lax.rem(osi, NC)
    half = nz // 2
    rows_k = nz * cap
    chunk = NY * rows_k // (NC * nx)
    tok_n = tok.shape[0]
    started = []

    def dev(dz=0, dy=0, dx=0, other=False):
        e = lax.rem(z + dz + nz, nz) * NY + lax.rem(y + dy + NY, NY)
        o = lax.rem(x + dx + nx, nx) * NC + ((1 - c) if other else c)
        return (e, o)

    flip = 1 - 2 * lax.rem(y, 2)
    pair_y = (z * NY + y + flip, osi)

    def send(src, dst, sem, idx, to):
        cp = pltpu.make_async_remote_copy(
            src_ref=src,
            dst_ref=dst,
            send_sem=sem.at[(0,) + idx],
            recv_sem=sem.at[(1,) + idx],
            device_id=to,
            device_id_type=MESH,
        )
        cp.start()
        started.append(cp)
        return cp

    loc = [
        pltpu.make_async_copy(tok, tc.at[half - 1, 1, 0], s_loc.at[0]),
        pltpu.make_async_copy(cot, tc.at[half - 1, 1, 1], s_loc.at[1]),
    ]
    for cp in loc:
        cp.start()
    mt[half - 1, 1, 0:8] = ids[...].astype(F32)
    mt[half - 1, 1, 8:16] = rw[...]

    peers = [dev(dz=1), dev(dz=-1), dev(dz=half)]
    peers += [dev(dy=k) for k in range(1, NY)]
    peers += [dev(dx=m) for m in range(1, nx)]
    peers += [dev(other=True)]
    barrier = pltpu.get_barrier_semaphore()
    for d in peers:
        pl.semaphore_signal(barrier, inc=1, device_id=d, device_id_type=MESH)
    pl.semaphore_wait(barrier, len(peers))
    for cp in loc:
        cp.wait()

    ag = {}

    def ag_send(s, d):
        src = (half - 1, 1) if s == 0 else (s - 1, d)
        to = dev(dz=1 if d == 0 else -1)
        ag[s, d] = (
            send(tc.at[src], tc.at[s, d], s_ag, (0, d, s), to),
            send(mt.at[src], mt.at[s, d], s_ag, (1, d, s), to),
        )

    ag_send(0, 0)
    ag_send(0, 1)
    state = (par, mom1, mom2)
    ycp = [send(state[a], yb.at[a], s_y, (a,), pair_y) for a in range(3)]

    def held(i, iy):
        f1 = flags[1, i] == 1
        zi = lax.rem(i + half * NY, nz * NY)
        ziy = lax.rem(iy + half * NY, nz * NY)
        stay = jnp.where(flags[0, i] == 1, place[zi], place[i])
        move = jnp.where(flags[0, iy] == 1, place[ziy], place[iy])
        return jnp.where(f1, move, stay)

    experts = []
    for k in range(NY):
        yk = lax.rem(y + k, NY)
        i = z * NY + yk
        experts.append(held(i, i + 1 - 2 * lax.rem(yk, 2)).astype(F32))
    i_y = z * NY + y + flip
    i_z = lax.rem(ep + half * NY, nz * NY)
    f1_own = flags[1, ep] == 1
    f1_far = flags[1, i_z] == 1
    from_far = jnp.where(f1_own, flags[0, i_y], flags[0, ep]) == 1

    tri = (
        lax.broadcasted_iota(jnp.int32, (tok_n, tok_n), 0)
        < lax.broadcasted_iota(jnp.int32, (tok_n, tok_n), 1)
    ).astype(F32).astype(BF16)
    slots = lax.broadcasted_iota(jnp.int32, (cap, tok_n), 0).astype(F32)
    nothing = jnp.zeros((cap, tok_n), F32)

    def route(s):
        hits, weights = [], []
        for k in range(NY):
            for b in range(2):
                hit = jnp.where(mt[s, b, 0:8] == experts[k], 1.0, 0.0)
                hits.append(jnp.sum(hit, axis=0, keepdims=True))
                weights.append(jnp.sum(hit * mt[s, b, 8:16], axis=0, keepdims=True))
        mask = jnp.concatenate(hits, axis=0)
        slot = dot(mask.astype(BF16), tri)
        pick, pick_w = [], []
        for k in range(NY):
            for b in range(2):
                r = 2 * k + b
                keep = mask[r : r + 1] > 0.5
                one = jnp.where((slots == slot[r : r + 1]) & keep, 1.0, 0.0)
                w = one * weights[r]
                pick.append(jnp.concatenate((one, nothing) if b == 0 else (nothing, one), axis=1))
                pick_w.append(jnp.concatenate((w, nothing) if b == 0 else (nothing, w), axis=1))
        ones = jnp.concatenate(pick, axis=0).astype(BF16)
        wide = jnp.concatenate(pick_w, axis=0)
        high = wide.astype(BF16)
        p01[s] = ones
        phi[s] = high
        plo[s] = (wide - high.astype(F32)).astype(BF16)
        scale = jnp.sum(wide, axis=1, keepdims=True)
        t_in = jnp.concatenate((tc[s, 0, 0], tc[s, 1, 0]), axis=0)
        c_in = jnp.concatenate((tc[s, 0, 1], tc[s, 1, 1]), axis=0)
        picked = (dot(ones, t_in).astype(BF16), (scale * dot(ones, c_in)).astype(BF16))
        width = 2 * cap
        for a in range(2):
            for k in range(NY):
                part = picked[a][k * width : (k + 1) * width]
                if k == 0:
                    rx[a, 0, s * width : (s + 1) * width] = part
                else:
                    sx[a, k - 1, s * width : (s + 1) * width] = part

    for s in range(half):
        for d in range(2):
            if (s, d) not in ag:
                continue
            for cp in ag[s, d]:
                cp.wait_recv()
            if s + 1 < half - d:
                ag_send(s + 1, d)
        if s == half - 2:
            ycp[0].wait_recv()
            zs[0] = jnp.where(f1_far, yb[0], par[...])
        if s + 1 == half:
            zcp = [send(zs.at[0], zr.at[0], s_z, (0,), dev(dz=half))]
        route(s)

    rcp = {}
    for a in range(2):
        for k in range(1, NY):
            rcp[a, k] = send(sx.at[a, k - 1], rx.at[a, k], s_yx, (a, k - 1), dev(dy=k))
    for a in (1, 2):
        ycp[a].wait_recv()
        zs[a] = jnp.where(f1_far, yb[a], state[a][...])
        zcp.append(send(zs.at[a], zr.at[a], s_z, (a,), dev(dz=half)))

    for cp in rcp.values():
        cp.wait_recv()
    zcp[0].wait_recv()
    wf[...] = jnp.where(from_far, zr[0], jnp.where(f1_own, yb[0], par[...]))

    per = rows_k // chunk
    base_o, base_c = (1 - c) * (NY // NC), c * (NY // NC)
    ccp = []
    for arr in range(3):
        which = 0 if arr < 2 else 1
        for xi in range(nx):
            rows = rx[which, base_o + xi // per, (xi % per) * chunk : (xi % per + 1) * chunk]
            psnd[arr, xi] = dot(rows, wf[arr]).astype(BF16)
        ccp.append(send(psnd.at[arr], crecv.at[arr], s_c, (arr,), dev(other=True)))
    for arr in range(3):
        which = 0 if arr < 2 else 1
        for xi in range(nx):
            rows = rx[which, base_c + xi // per, (xi % per) * chunk : (xi % per + 1) * chunk]
            own[arr, xi] = dot(rows, wf[arr])
    xcp = {}
    sums = []
    for arr in range(3):
        ccp[arr].wait_recv()
        for m in range(1, nx):
            xi = lax.rem(x + m, nx)
            xs[m - 1, arr] = (own[arr, xi] + crecv[arr, xi].astype(F32)).astype(BF16)
            xcp[arr, m] = send(xs.at[m - 1, arr], xr.at[m - 1, arr], s_x, (arr, m - 1), dev(dx=m))

    def total(arr):
        acc = own[arr, x] + crecv[arr, x].astype(F32)
        for m in range(1, nx):
            xcp[arr, m].wait_recv()
            acc = acc + xr[m - 1, arr].astype(F32)
        return acc

    hcp = {}

    def spread(a):
        for m in range(1, nx):
            hcp[a, m] = send(hh.at[a, c, x], hh.at[a, c, x], s_h, (a, m - 1), dev(dx=m))
        hcp[a, 0] = send(hh.at[a, c, x], hh.at[a, c, x], s_hc, (a, 0), dev(other=True))

    own[0, x] = total(0)
    own[1, x] = total(1)
    gate, up = own[0, x], own[1, x]
    hh[0, c, x] = (gate * jax.nn.sigmoid(gate) * up).astype(BF16)
    spread(0)
    own[2, x] = total(2)
    gate, up, back = own[0, x], own[1, x], own[2, x]
    sigma = jax.nn.sigmoid(gate)
    hh[1, c, x] = (back * up * sigma * (1.0 + gate * (1.0 - sigma))).astype(BF16)
    hh[2, c, x] = (back * (gate * sigma)).astype(BF16)
    spread(1)
    spread(2)

    fcp = {}

    def forward(a):
        for m in range(1, nx):
            hcp[a, m].wait_recv()
            xi = lax.rem(x - m + nx, nx)
            fcp[a, m] = send(hh.at[a, c, xi], hh.at[a, c, xi], s_hc, (a, m), dev(other=True))

    def arrived(a):
        hcp[a, 0].wait_recv()
        for m in range(1, nx):
            fcp[a, m].wait_recv()

    bcp = {}

    def part(a, k):
        return hh[a, k // (NY // NC), (k % (NY // NC)) * per : (k % (NY // NC) + 1) * per].reshape(rows_k, -1)

    def give_back(a, k, value):
        if k == 0:
            yr[a, 0] = value
        else:
            yo[a, k - 1] = value
            bcp[a, k] = send(yo.at[a, k - 1], yr.at[a, k], s_yo, (a, k - 1), dev(dy=-k))

    forward(0)
    arrived(0)
    for k in (2, 1, 3, 0):
        give_back(0, k, dot_nt(part(0, k), wf[2]).astype(BF16))
    forward(1)
    forward(2)
    arrived(1)
    arrived(2)
    for k in (2, 1, 3, 0):
        value = dot_nt(part(1, k), wf[0]) + dot_nt(part(2, k), wf[1])
        give_back(1, k, value.astype(BF16))

    for which, a, out in ((0, 1, 0), (0, 2, 1), (1, 0, 2)):
        for k in range(NY):
            term = dot_tn(rx[which, k], part(a, k))
            gr[out] = term if k == 0 else gr[out] + term

    width = 2 * cap

    def combine(a):
        for k in range(1, NY):
            bcp[a, k].wait_recv()
        for s in range(half - 1, -1, -1):
            rows = jnp.concatenate([yr[a, k, s * width : (s + 1) * width] for k in range(NY)], axis=0)
            if a == 0:
                value = dot_tn(phi[s], rows) + dot_tn(plo[s], rows)
            else:
                value = dot_tn(p01[s], rows)
            prt[a, s, 0] = value[:tok_n]
            prt[a, s, 1] = value[tok_n:]

    combine(0)
    combine(1)
    last = {}
    for t in range(half):
        for a in range(2):
            for d in range(2):
                steps = half - d
                if t >= steps:
                    continue
                value = prt[a, steps - 1 - t, d]
                if t:
                    last[a, d].wait_recv()
                    value = value + rsr[a, d, t - 1].astype(F32)
                rss[a, d, t] = value.astype(BF16)
                last[a, d] = send(
                    rss.at[a, d, t], rsr.at[a, d, t], s_rs, (a, d, t), dev(dz=-1 if d == 0 else 1)
                )
    for a, out in ((0, mixed), (1, igrad)):
        value = prt[a, half - 1, 1]
        for d in range(2):
            last[a, d].wait_recv()
            value = value + rsr[a, d, half - d - 1].astype(F32)
        out[...] = value.astype(BF16)

    zcp[1].wait_recv()
    zcp[2].wait_recv()
    for k in range(3):
        grad = gr[k]
        first = jnp.where(from_far, zr[1, k], jnp.where(f1_own, yb[1, k], mom1[k])).astype(F32)
        second = jnp.where(from_far, zr[2, k], jnp.where(f1_own, yb[2, k], mom2[k])).astype(F32)
        first = beta_first * first + (1.0 - beta_first) * grad
        second = beta_second * second + (1.0 - beta_second) * grad * grad
        new_m[k] = first.astype(BF16)
        new_v[k] = second.astype(BF16)
        first_hat = first * (1.0 / (1.0 - beta_first**adam_count))
        second_hat = second * (1.0 / (1.0 - beta_second**adam_count))
        new_p[k] = (
            wf[k].astype(F32) - learn_rate * first_hat / (jnp.sqrt(second_hat) + adam_eps)
        ).astype(BF16)

    for cp in started:
        cp.wait_send()


def on_device(tokens, cotangent, expert_ids, route_weight, placement, swap_flags, params, first_moment, second_moment):
    nz = lax.axis_size("ep") // NY
    nx = lax.axis_size("os") // NC
    tok_n, shard = tokens.shape
    top = expert_ids.shape[1]
    _, _, _, hw = params.shape
    cap = max(2, 3 * tok_n * top // (2 * lax.axis_size("ep")))
    half = nz // 2
    rows_k = nz * cap
    chunk = NY * rows_k // (NC * nx)
    vmem = pl.BlockSpec(memory_space=pltpu.VMEM)
    smem = pl.BlockSpec(memory_space=pltpu.SMEM)
    anywhere = pl.BlockSpec(memory_space=pl.ANY)
    mat = (3, shard, hw)
    dma = pltpu.SemaphoreType.DMA
    pick = (half, NY * 2 * cap, 2 * tok_n)
    scratch = [
        pltpu.VMEM((half, 2, 2, tok_n, shard), BF16),
        pltpu.VMEM((half, 2, 2 * top, tok_n), F32),
        pltpu.VMEM((3,) + mat, BF16),
        pltpu.VMEM((3,) + mat, BF16),
        pltpu.VMEM((3,) + mat, BF16),
        pltpu.VMEM(mat, BF16),
        pltpu.VMEM((2, NY - 1, rows_k, shard), BF16),
        pltpu.VMEM((2, NY, rows_k, shard), BF16),
        pltpu.VMEM(pick, BF16),
        pltpu.VMEM(pick, BF16),
        pltpu.VMEM(pick, BF16),
        pltpu.VMEM((3, nx, chunk, hw), BF16),
        pltpu.VMEM((3, nx, chunk, hw), F32),
        pltpu.VMEM((3, nx, chunk, hw), BF16),
        pltpu.VMEM((nx - 1, 3, chunk, hw), BF16),
        pltpu.VMEM((nx - 1, 3, chunk, hw), BF16),
        pltpu.VMEM((3, NC, nx, chunk, hw), BF16),
        pltpu.VMEM((2, NY - 1, rows_k, shard), BF16),
        pltpu.VMEM((2, NY, rows_k, shard), BF16),
        pltpu.VMEM((2, half, 2, tok_n, shard), F32),
        pltpu.VMEM((2, 2, half, tok_n, shard), BF16),
        pltpu.VMEM((2, 2, half, tok_n, shard), BF16),
        pltpu.VMEM(mat, F32),
        dma((2,)),
        dma((2, 2, 2, half)),
        dma((2, 3)),
        dma((2, 3)),
        dma((2, 2, NY - 1)),
        dma((2, 3)),
        dma((2, 3, nx - 1)),
        dma((2, 3, nx - 1)),
        dma((2, 3, nx)),
        dma((2, 2, NY - 1)),
        dma((2, 2, 2, half)),
    ]
    out = pl.pallas_call(
        functools.partial(kernel, nz, nx, cap),
        name="expert_step",
        out_shape=(
            jax.ShapeDtypeStruct((tok_n, shard), BF16),
            jax.ShapeDtypeStruct((tok_n, shard), BF16),
            jax.ShapeDtypeStruct(mat, BF16),
            jax.ShapeDtypeStruct(mat, BF16),
            jax.ShapeDtypeStruct(mat, BF16),
        ),
        in_specs=[smem, smem, vmem, vmem, anywhere, anywhere, vmem, vmem, vmem],
        out_specs=(vmem,) * 5,
        scratch_shapes=scratch,
        compiler_params=pltpu.CompilerParams(
            collective_id=0, has_side_effects=True, vmem_limit_bytes=66 * 1000 * 1000
        ),
    )(
        placement,
        swap_flags,
        expert_ids.T,
        route_weight.T,
        tokens,
        cotangent,
        params[0],
        first_moment[0],
        second_moment[0],
    )
    return (out[0], out[1], out[2][None], out[3][None], out[4][None])


def solution(mesh):
    wide = P("ep", None, "os", None)
    placed = (P("ep", "os"), P("ep", "os"), P("ep", None), P("ep", None), P(), P(), wide, wide, wide)
    return jax.shard_map(
        on_device,
        mesh=mesh,
        in_specs=placed,
        out_specs=(P("ep", "os"), P("ep", "os"), wide, wide, wide),
        check_vma=False,
    )
```

```python
import functools

import jax
import jax.numpy as jnp
from jax import lax
from jax.experimental import pallas as pl
from jax.experimental.pallas import tpu as pltpu
from jax.sharding import PartitionSpec as P

MESH = pl.DeviceIdType.MESH
F32 = jnp.float32
BF16 = jnp.bfloat16

beta_first = 0.9
beta_second = 0.999
learn_rate = 0.01
adam_eps = 1e-08
adam_count = 10.0

RELAY = (3, 2, 7, 2, 7, 3, 5, 2)
NY = 4
NC = 2


def dot(a, b):
    return jnp.dot(a, b, preferred_element_type=F32)


def dot_nt(a, b):
    return lax.dot_general(a, b, (((1,), (1,)), ((), ())), preferred_element_type=F32)


def dot_tn(a, b):
    return lax.dot_general(a, b, (((0,), (0,)), ((), ())), preferred_element_type=F32)


def kernel(
    nz,
    nx,
    cap,
    place,
    flags,
    ids,
    rw,
    tok,
    cot,
    par,
    mom1,
    mom2,
    mixed,
    igrad,
    grads,
    held_p,
    held_m,
    held_v,
    tc,
    mt,
    sb,
    hop,
    yb,
    zs,
    zr,
    sx,
    rx,
    p01,
    phi,
    plo,
    psnd,
    own,
    crecv,
    xs,
    xr,
    hh,
    yo,
    yr,
    prt,
    rss,
    rsr,
    s_loc,
    s_ag,
    s_y,
    s_z,
    s_yx,
    s_c,
    s_x,
    s_h,
    s_hc,
    s_yo,
    s_rs,
):
    ep = lax.axis_index("ep")
    osi = lax.axis_index("os")
    z, y = lax.div(ep, NY), lax.rem(ep, NY)
    x, c = lax.div(osi, NC), lax.rem(osi, NC)
    half = nz // 2
    rows_k = nz * cap
    chunk = NY * rows_k // (NC * nx)
    tok_n = tok.shape[0]
    started = []

    def dev(dz=0, dy=0, dx=0, other=False):
        e = lax.rem(z + dz + nz, nz) * NY + lax.rem(y + dy + NY, NY)
        o = lax.rem(x + dx + nx, nx) * NC + ((1 - c) if other else c)
        return (e, o)

    flip = 1 - 2 * lax.rem(y, 2)
    pair_y = (z * NY + y + flip, osi)

    def send(src, dst, sem, idx, to):
        cp = pltpu.make_async_remote_copy(
            src_ref=src,
            dst_ref=dst,
            send_sem=sem.at[(0,) + idx],
            recv_sem=sem.at[(1,) + idx],
            device_id=to,
            device_id_type=MESH,
        )
        cp.start()
        started.append(cp)
        return cp

    loc = [
        pltpu.make_async_copy(tok, tc.at[half - 1, 1, 0], s_loc.at[0]),
        pltpu.make_async_copy(cot, tc.at[half - 1, 1, 1], s_loc.at[1]),
    ]
    state = (par, mom1, mom2)
    loc += [pltpu.make_async_copy(state[a], sb.at[a], s_loc.at[2 + a]) for a in range(3)]
    for cp in loc:
        cp.start()
    mt[half - 1, 1, 0:8] = ids[...].astype(F32)
    mt[half - 1, 1, 8:16] = rw[...]

    peers = [dev(dz=1), dev(dz=-1), dev(dz=half)]
    peers += [dev(dy=k) for k in range(1, NY)]
    peers += [dev(dx=m) for m in range(1, nx)]
    peers += [dev(other=True)]
    barrier = pltpu.get_barrier_semaphore()
    for d in peers:
        pl.semaphore_signal(barrier, inc=1, device_id=d, device_id_type=MESH)
    pl.semaphore_wait(barrier, len(peers))
    for cp in loc[:3]:
        cp.wait()

    ag = {}

    def ag_send(s, d):
        src = (half - 1, 1) if s == 0 else (s - 1, d)
        to = dev(dz=1 if d == 0 else -1)
        ag[s, d] = (
            send(tc.at[src], tc.at[s, d], s_ag, (0, d, s), to),
            send(mt.at[src], mt.at[s, d], s_ag, (1, d, s), to),
        )

    ag_send(0, 0)
    ag_send(0, 1)
    ycp = {(0, m): send(sb.at[0, m], yb.at[0, m], s_y, (0, m), pair_y) for m in range(3)}
    for a in (1, 2):
        loc[2 + a].wait()
        for m in range(3):
            ycp[a, m] = send(sb.at[a, m], yb.at[a, m], s_y, (a, m), pair_y)

    def held(i, iy):
        f1 = flags[1, i] == 1
        zi = lax.rem(i + half * NY, nz * NY)
        ziy = lax.rem(iy + half * NY, nz * NY)
        stay = jnp.where(flags[0, i] == 1, place[zi], place[i])
        move = jnp.where(flags[0, iy] == 1, place[ziy], place[iy])
        return jnp.where(f1, move, stay)

    experts = []
    for k in range(NY):
        yk = lax.rem(y + k, NY)
        i = z * NY + yk
        experts.append(held(i, i + 1 - 2 * lax.rem(yk, 2)).astype(F32))
    i_y = z * NY + y + flip
    i_z = lax.rem(ep + half * NY, nz * NY)
    f1_own = flags[1, ep] == 1
    f1_far = flags[1, i_z] == 1
    from_far = jnp.where(f1_own, flags[0, i_y], flags[0, ep]) == 1

    tri = (
        lax.broadcasted_iota(jnp.int32, (tok_n, tok_n), 0)
        < lax.broadcasted_iota(jnp.int32, (tok_n, tok_n), 1)
    ).astype(F32).astype(BF16)
    slots = lax.broadcasted_iota(jnp.int32, (cap, tok_n), 0).astype(F32)
    nothing = jnp.zeros((cap, tok_n), F32)

    zcp = {}
    cut = par.shape[1] // 2

    def z_hop(a, m, h):
        if h == 0:
            ycp[a, m].wait_recv()
            zs[a, m] = jnp.where(f1_far, yb[a, m], sb[a, m])
        for d in range(2):
            piece = (a, m, pl.ds(d * cut, cut))
            if h:
                zcp[a, m, d, h - 1].wait_recv()
            src = zs.at[piece] if h == 0 else hop.at[(h - 1,) + piece]
            dst = zr.at[piece] if h == half - 1 else hop.at[(h,) + piece]
            zcp[a, m, d, h] = send(src, dst, s_z, (a, m, d, h), dev(dz=1 if d == 0 else -1))

    def z_wait(a):
        for m in range(3):
            for d in range(2):
                zcp[a, m, d, half - 1].wait_recv()

    def select(a, m):
        return jnp.where(from_far, zr[a, m], jnp.where(f1_own, yb[a, m], sb[a, m]))

    queue = [(a, m, h) for a in (1, 2) for h in range(half) for m in range(3)]

    def relay(count):
        for _ in range(min(count, len(queue))):
            z_hop(*queue.pop(0))

    def route(s):
        hits, weights = [], []
        for k in range(NY):
            for b in range(2):
                hit = jnp.where(mt[s, b, 0:8] == experts[k], 1.0, 0.0)
                hits.append(jnp.sum(hit, axis=0, keepdims=True))
                weights.append(jnp.sum(hit * mt[s, b, 8:16], axis=0, keepdims=True))
        mask = jnp.concatenate(hits, axis=0)
        slot = dot(mask.astype(BF16), tri)
        pick, pick_w = [], []
        for k in range(NY):
            for b in range(2):
                r = 2 * k + b
                keep = mask[r : r + 1] > 0.5
                one = jnp.where((slots == slot[r : r + 1]) & keep, 1.0, 0.0)
                w = one * weights[r]
                pick.append(jnp.concatenate((one, nothing) if b == 0 else (nothing, one), axis=1))
                pick_w.append(jnp.concatenate((w, nothing) if b == 0 else (nothing, w), axis=1))
        ones = jnp.concatenate(pick, axis=0).astype(BF16)
        wide = jnp.concatenate(pick_w, axis=0)
        high = wide.astype(BF16)
        p01[s] = ones
        phi[s] = high
        plo[s] = (wide - high.astype(F32)).astype(BF16)
        scale = jnp.sum(wide, axis=1, keepdims=True)
        t_in = jnp.concatenate((tc[s, 0, 0], tc[s, 1, 0]), axis=0)
        c_in = jnp.concatenate((tc[s, 0, 1], tc[s, 1, 1]), axis=0)
        picked = (dot(ones, t_in).astype(BF16), (scale * dot(ones, c_in)).astype(BF16))
        width = 2 * cap
        for a in range(2):
            for k in range(NY):
                part = picked[a][k * width : (k + 1) * width]
                if k == 0:
                    rx[a, 0, s * width : (s + 1) * width] = part
                else:
                    sx[a, k - 1, s * width : (s + 1) * width] = part

    rcp = []
    batch = 2
    width = 2 * cap
    for s in range(half + 1):
        for d in range(2):
            if (s, d) not in ag:
                continue
            for cp in ag[s, d]:
                cp.wait_recv()
            if s + 1 < half - d:
                ag_send(s + 1, d)
        if s > 0:
            for m in range(3):
                z_hop(0, m, s - 1)
        if s < half:
            route(s)
            if s % batch == batch - 1:
                b = s // batch
                piece = pl.ds(b * batch * width, batch * width)
                for a in range(2):
                    for k in range(1, NY):
                        rcp.append(
                            send(sx.at[a, k - 1, piece], rx.at[a, k, piece], s_yx, (a, k - 1, b), dev(dy=k))
                        )
    relay(RELAY[0])
    for cp in rcp:
        cp.wait_recv()
    z_wait(0)
    for m in range(3):
        held_p[m] = select(0, m)

    per = rows_k // chunk
    base_o, base_c = (1 - c) * (NY // NC), c * (NY // NC)
    ccp = []
    for arr in range(3):
        which = 0 if arr < 2 else 1
        for xi in range(nx):
            rows = rx[which, base_o + xi // per, (xi % per) * chunk : (xi % per + 1) * chunk]
            psnd[arr, xi] = dot(rows, held_p[arr]).astype(BF16)
        ccp.append(send(psnd.at[arr], crecv.at[arr], s_c, (arr,), dev(other=True)))
    relay(RELAY[1])
    for arr in range(3):
        which = 0 if arr < 2 else 1
        for xi in range(nx):
            rows = rx[which, base_c + xi // per, (xi % per) * chunk : (xi % per + 1) * chunk]
            own[arr, xi] = dot(rows, held_p[arr])
    xcp = {}
    sums = []
    for arr in range(3):
        ccp[arr].wait_recv()
        for m in range(1, nx):
            xi = lax.rem(x + m, nx)
            xs[m - 1, arr] = (own[arr, xi] + crecv[arr, xi].astype(F32)).astype(BF16)
            xcp[arr, m] = send(xs.at[m - 1, arr], xr.at[m - 1, arr], s_x, (arr, m - 1), dev(dx=m))

    relay(RELAY[2])

    def total(arr):
        acc = own[arr, x] + crecv[arr, x].astype(F32)
        for m in range(1, nx):
            xcp[arr, m].wait_recv()
            acc = acc + xr[m - 1, arr].astype(F32)
        return acc

    hcp = {}

    def spread(a):
        for m in range(1, nx):
            hcp[a, m] = send(hh.at[a, c, x], hh.at[a, c, x], s_h, (a, m - 1), dev(dx=m))
        hcp[a, 0] = send(hh.at[a, c, x], hh.at[a, c, x], s_hc, (a, 0), dev(other=True))

    own[0, x] = total(0)
    own[1, x] = total(1)
    gate, up = own[0, x], own[1, x]
    hh[0, c, x] = (gate * jax.nn.sigmoid(gate) * up).astype(BF16)
    spread(0)
    relay(RELAY[3])
    own[2, x] = total(2)
    gate, up, back = own[0, x], own[1, x], own[2, x]
    sigma = jax.nn.sigmoid(gate)
    hh[1, c, x] = (back * up * sigma * (1.0 + gate * (1.0 - sigma))).astype(BF16)
    hh[2, c, x] = (back * (gate * sigma)).astype(BF16)
    spread(1)
    spread(2)

    relay(RELAY[4])
    fcp = {}

    def forward(a):
        for m in range(1, nx):
            hcp[a, m].wait_recv()
            xi = lax.rem(x - m + nx, nx)
            fcp[a, m] = send(hh.at[a, c, xi], hh.at[a, c, xi], s_hc, (a, m), dev(other=True))

    def arrived(a):
        hcp[a, 0].wait_recv()
        for m in range(1, nx):
            fcp[a, m].wait_recv()

    bcp = {}

    def part(a, k):
        return hh[a, k // (NY // NC), (k % (NY // NC)) * per : (k % (NY // NC) + 1) * per].reshape(rows_k, -1)

    def give_back(a, k, value):
        if k == 0:
            yr[a, 0] = value
        else:
            yo[a, k - 1] = value
            bcp[a, k] = send(yo.at[a, k - 1], yr.at[a, k], s_yo, (a, k - 1), dev(dy=-k))

    forward(0)
    arrived(0)
    for k in (2, 1, 3, 0):
        give_back(0, k, dot_nt(part(0, k), held_p[2]).astype(BF16))
    relay(RELAY[5])
    forward(1)
    forward(2)
    arrived(1)
    arrived(2)
    for k in (2, 1, 3, 0):
        value = dot_nt(part(1, k), held_p[0]) + dot_nt(part(2, k), held_p[1])
        give_back(1, k, value.astype(BF16))

    for which, a, out in ((0, 1, 0), (0, 2, 1), (1, 0, 2)):
        for k in range(NY):
            term = dot_tn(rx[which, k], part(a, k))
            grads[out] = term if k == 0 else grads[out] + term

    relay(RELAY[6])
    def combine(a):
        for k in range(1, NY):
            bcp[a, k].wait_recv()
        for s in range(half - 1, -1, -1):
            rows = jnp.concatenate([yr[a, k, s * width : (s + 1) * width] for k in range(NY)], axis=0)
            if a == 0:
                value = dot_tn(phi[s], rows) + dot_tn(plo[s], rows)
            else:
                value = dot_tn(p01[s], rows)
            prt[a, s, 0] = value[:tok_n]
            prt[a, s, 1] = value[tok_n:]

    combine(0)
    combine(1)
    last = {}
    for t in range(half):
        for a in range(2):
            for d in range(2):
                steps = half - d
                if t >= steps:
                    continue
                value = prt[a, steps - 1 - t, d]
                if t:
                    last[a, d].wait_recv()
                    value = value + rsr[a, d, t - 1].astype(F32)
                rss[a, d, t] = value.astype(BF16)
                last[a, d] = send(
                    rss.at[a, d, t], rsr.at[a, d, t], s_rs, (a, d, t), dev(dz=-1 if d == 0 else 1)
                )
        relay(RELAY[7])
    relay(len(queue))
    for a, out in ((0, mixed), (1, igrad)):
        value = prt[a, half - 1, 1]
        for d in range(2):
            last[a, d].wait_recv()
            value = value + rsr[a, d, half - d - 1].astype(F32)
        out[...] = value.astype(BF16)

    for a, out in ((1, held_m), (2, held_v)):
        z_wait(a)
        for m in range(3):
            out[m] = select(a, m)

    for cp in started:
        cp.wait_send()


def adam_update(weight, first, second, grad):
    first_new = beta_first * first.astype(F32) + (1.0 - beta_first) * grad
    second_new = beta_second * second.astype(F32) + (1.0 - beta_second) * grad * grad
    first_hat = first_new / (1.0 - beta_first**adam_count)
    second_hat = second_new / (1.0 - beta_second**adam_count)
    weight_new = weight.astype(F32) - learn_rate * first_hat / (jnp.sqrt(second_hat) + adam_eps)
    return weight_new.astype(BF16), first_new.astype(BF16), second_new.astype(BF16)


def on_device(tokens, cotangent, expert_ids, route_weight, placement, swap_flags, params, first_moment, second_moment):
    nz = lax.axis_size("ep") // NY
    nx = lax.axis_size("os") // NC
    tok_n, shard = tokens.shape
    top = expert_ids.shape[1]
    _, _, _, hw = params.shape
    cap = max(2, 3 * tok_n * top // (2 * lax.axis_size("ep")))
    half = nz // 2
    rows_k = nz * cap
    chunk = NY * rows_k // (NC * nx)
    vmem = pl.BlockSpec(memory_space=pltpu.VMEM)
    smem = pl.BlockSpec(memory_space=pltpu.SMEM)
    anywhere = pl.BlockSpec(memory_space=pl.ANY)
    mat = (3, shard, hw)
    dma = pltpu.SemaphoreType.DMA
    pick = (half, NY * 2 * cap, 2 * tok_n)
    scratch = [
        pltpu.VMEM((half, 2, 2, tok_n, shard), BF16),
        pltpu.VMEM((half, 2, 2 * top, tok_n), F32),
        pltpu.VMEM((3,) + mat, BF16),
        pltpu.VMEM((half - 1, 3) + mat, BF16),
        pltpu.VMEM((3,) + mat, BF16),
        pltpu.VMEM((3,) + mat, BF16),
        pltpu.VMEM((3,) + mat, BF16),
        pltpu.VMEM((2, NY - 1, rows_k, shard), BF16),
        pltpu.VMEM((2, NY, rows_k, shard), BF16),
        pltpu.VMEM(pick, BF16),
        pltpu.VMEM(pick, BF16),
        pltpu.VMEM(pick, BF16),
        pltpu.VMEM((3, nx, chunk, hw), BF16),
        pltpu.VMEM((3, nx, chunk, hw), F32),
        pltpu.VMEM((3, nx, chunk, hw), BF16),
        pltpu.VMEM((nx - 1, 3, chunk, hw), BF16),
        pltpu.VMEM((nx - 1, 3, chunk, hw), BF16),
        pltpu.VMEM((3, NC, nx, chunk, hw), BF16),
        pltpu.VMEM((2, NY - 1, rows_k, shard), BF16),
        pltpu.VMEM((2, NY, rows_k, shard), BF16),
        pltpu.VMEM((2, half, 2, tok_n, shard), F32),
        pltpu.VMEM((2, 2, half, tok_n, shard), BF16),
        pltpu.VMEM((2, 2, half, tok_n, shard), BF16),
        dma((5,)),
        dma((2, 2, 2, half)),
        dma((2, 3, 3)),
        dma((2, 3, 3, 2, half)),
        dma((2, 2, NY - 1, half // 2)),
        dma((2, 3)),
        dma((2, 3, nx - 1)),
        dma((2, 3, nx - 1)),
        dma((2, 3, nx)),
        dma((2, 2, NY - 1)),
        dma((2, 2, 2, half)),
    ]
    out = pl.pallas_call(
        functools.partial(kernel, nz, nx, cap),
        name="expert_step",
        out_shape=(
            jax.ShapeDtypeStruct((tok_n, shard), BF16),
            jax.ShapeDtypeStruct((tok_n, shard), BF16),
            jax.ShapeDtypeStruct(mat, F32),
            jax.ShapeDtypeStruct(mat, BF16),
            jax.ShapeDtypeStruct(mat, BF16),
            jax.ShapeDtypeStruct(mat, BF16),
        ),
        in_specs=[smem, smem, vmem, vmem] + [anywhere] * 5,
        out_specs=(vmem,) * 6,
        scratch_shapes=scratch,
        compiler_params=pltpu.CompilerParams(
            collective_id=0, has_side_effects=True, vmem_limit_bytes=66 * 1000 * 1000
        ),
    )(
        placement,
        swap_flags,
        expert_ids.T,
        route_weight.T,
        tokens,
        cotangent,
        params[0],
        first_moment[0],
        second_moment[0],
    )
    mixed, input_grad, grad, *held = out
    updated = adam_update(*held, grad)
    return (mixed, input_grad, *(a[None] for a in updated))


def solution(mesh):
    wide = P("ep", None, "os", None)
    placed = (P("ep", "os"), P("ep", "os"), P("ep", None), P("ep", None), P(), P(), wide, wide, wide)
    return jax.shard_map(
        on_device,
        mesh=mesh,
        in_specs=placed,
        out_specs=(P("ep", "os"), P("ep", "os"), wide, wide, wide),
        check_vma=False,
    )
```

```python
import functools

import jax
import jax.numpy as jnp
from jax import lax
from jax.experimental import pallas as pl
from jax.experimental.pallas import tpu as pltpu
from jax.sharding import PartitionSpec as P

MESH = pl.DeviceIdType.MESH
F32 = jnp.float32
BF16 = jnp.bfloat16

beta_first = 0.9
beta_second = 0.999
learn_rate = 0.01
adam_eps = 1e-08
adam_count = 10.0

RELAY = (4, 2, 8, 3, 8, 3, 5, 2)
NY = 4
NC = 2


def dot(a, b):
    return jnp.dot(a, b, preferred_element_type=F32)


def dot_nt(a, b):
    return lax.dot_general(a, b, (((1,), (1,)), ((), ())), preferred_element_type=F32)


def dot_tn(a, b):
    return lax.dot_general(a, b, (((0,), (0,)), ((), ())), preferred_element_type=F32)


def kernel(
    nz,
    nx,
    cap,
    place,
    flags,
    ids,
    rw,
    tok,
    cot,
    par,
    mom1,
    mom2,
    mixed,
    igrad,
    grads,
    held_p,
    held_m,
    held_v,
    tc,
    mt,
    sb,
    hop,
    yb,
    zs,
    zr,
    sx,
    rx,
    p01,
    phi,
    plo,
    psnd,
    own,
    crecv,
    xs,
    xr,
    hh,
    yo,
    yr,
    prt,
    rss,
    rsr,
    s_loc,
    s_ag,
    s_y,
    s_z,
    s_yx,
    s_c,
    s_x,
    s_h,
    s_hc,
    s_yo,
    s_rs,
):
    ep = lax.axis_index("ep")
    osi = lax.axis_index("os")
    z, y = lax.div(ep, NY), lax.rem(ep, NY)
    x, c = lax.div(osi, NC), lax.rem(osi, NC)
    half = nz // 2
    rows_k = nz * cap
    chunk = NY * rows_k // (NC * nx)
    tok_n = tok.shape[0]
    started = []

    def dev(dz=0, dy=0, dx=0, other=False):
        e = lax.rem(z + dz + nz, nz) * NY + lax.rem(y + dy + NY, NY)
        o = lax.rem(x + dx + nx, nx) * NC + ((1 - c) if other else c)
        return (e, o)

    flip = 1 - 2 * lax.rem(y, 2)
    pair_y = (z * NY + y + flip, osi)

    def send(src, dst, sem, idx, to):
        cp = pltpu.make_async_remote_copy(
            src_ref=src,
            dst_ref=dst,
            send_sem=sem.at[(0,) + idx],
            recv_sem=sem.at[(1,) + idx],
            device_id=to,
            device_id_type=MESH,
        )
        cp.start()
        started.append(cp)
        return cp

    loc = [
        pltpu.make_async_copy(tok, tc.at[half - 1, 1, 0], s_loc.at[0]),
        pltpu.make_async_copy(cot, tc.at[half - 1, 1, 1], s_loc.at[1]),
    ]
    state = (par, mom1, mom2)
    loc += [pltpu.make_async_copy(state[a], sb.at[a], s_loc.at[2 + a]) for a in range(3)]
    for cp in loc:
        cp.start()
    mt[half - 1, 1, 0:8] = ids[...].astype(F32)
    mt[half - 1, 1, 8:16] = rw[...]

    peers = [dev(dz=1), dev(dz=-1)]
    peers += [dev(dy=k) for k in range(1, NY)]
    peers += [dev(dx=m) for m in range(1, nx)]
    peers += [dev(other=True)]
    barrier = pltpu.get_barrier_semaphore()
    for d in peers:
        pl.semaphore_signal(barrier, inc=1, device_id=d, device_id_type=MESH)
    pl.semaphore_wait(barrier, len(peers))
    for cp in loc[:3]:
        cp.wait()

    ag = {}

    def ag_send(s, d, part):
        src = (half - 1, 1) if s == 0 else (s - 1, d)
        ref, tail = (tc, (part,)) if part < 2 else (mt, ())
        ag[s, d, part] = send(
            ref.at[src + tail], ref.at[(s, d) + tail], s_ag, (part, d, s), dev(dz=1 if d == 0 else -1)
        )

    parts = (0, 2, 1)
    for part in parts:
        for d in range(2):
            ag_send(0, d, part)
    ycp = {(0, m): send(sb.at[0, m], yb.at[0, m], s_y, (0, m), pair_y) for m in range(3)}
    for a in (1, 2):
        loc[2 + a].wait()
        for m in range(3):
            ycp[a, m] = send(sb.at[a, m], yb.at[a, m], s_y, (a, m), pair_y)

    def held(i, iy):
        f1 = flags[1, i] == 1
        zi = lax.rem(i + half * NY, nz * NY)
        ziy = lax.rem(iy + half * NY, nz * NY)
        stay = jnp.where(flags[0, i] == 1, place[zi], place[i])
        move = jnp.where(flags[0, iy] == 1, place[ziy], place[iy])
        return jnp.where(f1, move, stay)

    experts = []
    for k in range(NY):
        yk = lax.rem(y + k, NY)
        i = z * NY + yk
        experts.append(held(i, i + 1 - 2 * lax.rem(yk, 2)).astype(F32))
    i_y = z * NY + y + flip
    i_z = lax.rem(ep + half * NY, nz * NY)
    f1_own = flags[1, ep] == 1
    f1_far = flags[1, i_z] == 1
    from_far = jnp.where(f1_own, flags[0, i_y], flags[0, ep]) == 1

    tri = (
        lax.broadcasted_iota(jnp.int32, (tok_n, tok_n), 0)
        < lax.broadcasted_iota(jnp.int32, (tok_n, tok_n), 1)
    ).astype(F32).astype(BF16)
    slots = lax.broadcasted_iota(jnp.int32, (cap, tok_n), 0).astype(F32)
    nothing = jnp.zeros((cap, tok_n), F32)

    zcp = {}
    cut = par.shape[1] // 2

    def z_hop(a, m, h):
        if h == 0:
            ycp[a, m].wait_recv()
            zs[a, m] = jnp.where(f1_far, yb[a, m], sb[a, m])
        for d in range(2):
            piece = (a, m, pl.ds(d * cut, cut))
            if h:
                zcp[a, m, d, h - 1].wait_recv()
            src = zs.at[piece] if h == 0 else hop.at[(h - 1,) + piece]
            dst = zr.at[piece] if h == half - 1 else hop.at[(h,) + piece]
            zcp[a, m, d, h] = send(src, dst, s_z, (a, m, d, h), dev(dz=1 if d == 0 else -1))

    def z_wait(a):
        for m in range(3):
            for d in range(2):
                zcp[a, m, d, half - 1].wait_recv()

    def select(a, m):
        return jnp.where(from_far, zr[a, m], jnp.where(f1_own, yb[a, m], sb[a, m]))

    queue = [(a, m, h) for a in (1, 2) for h in range(half) for m in range(3)]

    def relay(count):
        for _ in range(min(count, len(queue))):
            z_hop(*queue.pop(0))

    def route(s):
        hits, weights = [], []
        for k in range(NY):
            for b in range(2):
                hit = jnp.where(mt[s, b, 0:8] == experts[k], 1.0, 0.0)
                hits.append(jnp.sum(hit, axis=0, keepdims=True))
                weights.append(jnp.sum(hit * mt[s, b, 8:16], axis=0, keepdims=True))
        mask = jnp.concatenate(hits, axis=0)
        slot = dot(mask.astype(BF16), tri)
        pick, pick_w = [], []
        for k in range(NY):
            for b in range(2):
                r = 2 * k + b
                keep = mask[r : r + 1] > 0.5
                one = jnp.where((slots == slot[r : r + 1]) & keep, 1.0, 0.0)
                w = one * weights[r]
                pick.append(jnp.concatenate((one, nothing) if b == 0 else (nothing, one), axis=1))
                pick_w.append(jnp.concatenate((w, nothing) if b == 0 else (nothing, w), axis=1))
        ones = jnp.concatenate(pick, axis=0).astype(BF16)
        wide = jnp.concatenate(pick_w, axis=0)
        high = wide.astype(BF16)
        p01[s] = ones
        phi[s] = high
        plo[s] = (wide - high.astype(F32)).astype(BF16)
        scale = jnp.sum(wide, axis=1, keepdims=True)
        t_in = jnp.concatenate((tc[s, 0, 0], tc[s, 1, 0]), axis=0)
        c_in = jnp.concatenate((tc[s, 0, 1], tc[s, 1, 1]), axis=0)
        picked = (dot(ones, t_in).astype(BF16), (scale * dot(ones, c_in)).astype(BF16))
        width = 2 * cap
        for a in range(2):
            for k in range(NY):
                part = picked[a][k * width : (k + 1) * width]
                if k == 0:
                    rx[a, 0, s * width : (s + 1) * width] = part
                else:
                    sx[a, k - 1, s * width : (s + 1) * width] = part

    rcp = []
    batch = 2
    width = 2 * cap
    for s in range(half + 1):
        for part in parts:
            for d in range(2):
                if (s, d, part) not in ag:
                    continue
                ag[s, d, part].wait_recv()
                if s + 1 < half - d:
                    ag_send(s + 1, d, part)
        if s > 0:
            for m in range(3):
                z_hop(0, m, s - 1)
        if s < half:
            route(s)
            if s % batch == batch - 1:
                b = s // batch
                piece = pl.ds(b * batch * width, batch * width)
                for a in range(2):
                    for k in range(1, NY):
                        rcp.append(
                            send(sx.at[a, k - 1, piece], rx.at[a, k, piece], s_yx, (a, k - 1, b), dev(dy=k))
                        )
    relay(RELAY[0])
    for cp in rcp:
        cp.wait_recv()
    z_wait(0)
    for m in range(3):
        held_p[m] = select(0, m)

    per = rows_k // chunk
    base_o, base_c = (1 - c) * (NY // NC), c * (NY // NC)
    ccp = []
    for arr in range(3):
        which = 0 if arr < 2 else 1
        for xi in range(nx):
            rows = rx[which, base_o + xi // per, (xi % per) * chunk : (xi % per + 1) * chunk]
            psnd[arr, xi] = dot(rows, held_p[arr]).astype(BF16)
        ccp.append(send(psnd.at[arr], crecv.at[arr], s_c, (arr,), dev(other=True)))
    relay(RELAY[1])
    for arr in range(3):
        which = 0 if arr < 2 else 1
        for xi in range(nx):
            rows = rx[which, base_c + xi // per, (xi % per) * chunk : (xi % per + 1) * chunk]
            own[arr, xi] = dot(rows, held_p[arr])
    xcp = {}
    sums = []
    for arr in range(3):
        ccp[arr].wait_recv()
        for m in range(1, nx):
            xi = lax.rem(x + m, nx)
            xs[m - 1, arr] = (own[arr, xi] + crecv[arr, xi].astype(F32)).astype(BF16)
            xcp[arr, m] = send(xs.at[m - 1, arr], xr.at[m - 1, arr], s_x, (arr, m - 1), dev(dx=m))

    relay(RELAY[2])

    def total(arr):
        acc = own[arr, x] + crecv[arr, x].astype(F32)
        for m in range(1, nx):
            xcp[arr, m].wait_recv()
            acc = acc + xr[m - 1, arr].astype(F32)
        return acc

    hcp = {}

    def spread(a):
        for m in range(1, nx):
            hcp[a, m] = send(hh.at[a, c, x], hh.at[a, c, x], s_h, (a, m - 1), dev(dx=m))
        hcp[a, 0] = send(hh.at[a, c, x], hh.at[a, c, x], s_hc, (a, 0), dev(other=True))

    own[0, x] = total(0)
    own[1, x] = total(1)
    gate, up = own[0, x], own[1, x]
    hh[0, c, x] = (gate * jax.nn.sigmoid(gate) * up).astype(BF16)
    spread(0)
    relay(RELAY[3])
    own[2, x] = total(2)
    gate, up, back = own[0, x], own[1, x], own[2, x]
    sigma = jax.nn.sigmoid(gate)
    hh[1, c, x] = (back * up * sigma * (1.0 + gate * (1.0 - sigma))).astype(BF16)
    hh[2, c, x] = (back * (gate * sigma)).astype(BF16)
    spread(1)
    spread(2)

    relay(RELAY[4])
    fcp = {}

    def forward(a):
        for m in range(1, nx):
            hcp[a, m].wait_recv()
            xi = lax.rem(x - m + nx, nx)
            fcp[a, m] = send(hh.at[a, c, xi], hh.at[a, c, xi], s_hc, (a, m), dev(other=True))

    def arrived(a):
        hcp[a, 0].wait_recv()
        for m in range(1, nx):
            fcp[a, m].wait_recv()

    bcp = {}

    def part(a, k):
        return hh[a, k // (NY // NC), (k % (NY // NC)) * per : (k % (NY // NC) + 1) * per].reshape(rows_k, -1)

    def give_back(a, k, value):
        if k == 0:
            yr[a, 0] = value
        else:
            yo[a, k - 1] = value
            bcp[a, k] = send(yo.at[a, k - 1], yr.at[a, k], s_yo, (a, k - 1), dev(dy=-k))

    forward(0)
    arrived(0)
    for k in (2, 1, 3, 0):
        give_back(0, k, dot_nt(part(0, k), held_p[2]).astype(BF16))
    relay(RELAY[5])
    forward(1)
    forward(2)
    arrived(1)
    arrived(2)
    for k in (2, 1, 3, 0):
        value = dot_nt(part(1, k), held_p[0]) + dot_nt(part(2, k), held_p[1])
        give_back(1, k, value.astype(BF16))

    for which, a, out in ((0, 1, 0), (0, 2, 1), (1, 0, 2)):
        for k in range(NY):
            term = dot_tn(rx[which, k], part(a, k))
            grads[out] = term if k == 0 else grads[out] + term

    relay(RELAY[6])
    def combine(a):
        for k in range(1, NY):
            bcp[a, k].wait_recv()
        for s in range(half - 1, -1, -1):
            rows = jnp.concatenate([yr[a, k, s * width : (s + 1) * width] for k in range(NY)], axis=0)
            if a == 0:
                value = dot_tn(phi[s], rows) + dot_tn(plo[s], rows)
            else:
                value = dot_tn(p01[s], rows)
            prt[a, s, 0] = value[:tok_n]
            prt[a, s, 1] = value[tok_n:]

    combine(0)
    combine(1)
    last = {}
    for t in range(half):
        for a in range(2):
            for d in range(2):
                steps = half - d
                if t >= steps:
                    continue
                value = prt[a, steps - 1 - t, d]
                if t:
                    last[a, d].wait_recv()
                    value = value + rsr[a, d, t - 1].astype(F32)
                rss[a, d, t] = value.astype(BF16)
                last[a, d] = send(
                    rss.at[a, d, t], rsr.at[a, d, t], s_rs, (a, d, t), dev(dz=-1 if d == 0 else 1)
                )
        relay(RELAY[7])
    relay(len(queue))
    for a, out in ((0, mixed), (1, igrad)):
        value = prt[a, half - 1, 1]
        for d in range(2):
            last[a, d].wait_recv()
            value = value + rsr[a, d, half - d - 1].astype(F32)
        out[...] = value.astype(BF16)

    for a, out in ((1, held_m), (2, held_v)):
        z_wait(a)
        for m in range(3):
            out[m] = select(a, m)

    for cp in started:
        cp.wait_send()


def adam(grad, weight, first, second, mixed_in, input_in, new_p, new_m, new_v, mixed, igrad):
    @pl.when(pl.program_id(0) == 0)
    def _():
        mixed[...] = mixed_in[...]
        igrad[...] = input_in[...]

    g = grad[...]
    m = beta_first * first[...].astype(F32) + (1.0 - beta_first) * g
    v = beta_second * second[...].astype(F32) + (1.0 - beta_second) * g * g
    new_m[...] = m.astype(BF16)
    new_v[...] = v.astype(BF16)
    first_hat = m * (1.0 / (1.0 - beta_first**adam_count))
    second_hat = v * (1.0 / (1.0 - beta_second**adam_count))
    step = learn_rate * first_hat / (jnp.sqrt(second_hat) + adam_eps)
    new_p[...] = (weight[...].astype(F32) - step).astype(BF16)


ADAM_CUT = 1


def on_device(tokens, cotangent, expert_ids, route_weight, placement, swap_flags, params, first_moment, second_moment):
    nz = lax.axis_size("ep") // NY
    nx = lax.axis_size("os") // NC
    tok_n, shard = tokens.shape
    top = expert_ids.shape[1]
    _, _, _, hw = params.shape
    cap = max(2, 3 * tok_n * top // (2 * lax.axis_size("ep")))
    half = nz // 2
    rows_k = nz * cap
    chunk = NY * rows_k // (NC * nx)
    vmem = pl.BlockSpec(memory_space=pltpu.VMEM)
    smem = pl.BlockSpec(memory_space=pltpu.SMEM)
    anywhere = pl.BlockSpec(memory_space=pl.ANY)
    mat = (3, shard, hw)
    dma = pltpu.SemaphoreType.DMA
    pick = (half, NY * 2 * cap, 2 * tok_n)
    scratch = [
        pltpu.VMEM((half, 2, 2, tok_n, shard), BF16),
        pltpu.VMEM((half, 2, 2 * top, tok_n), F32),
        pltpu.VMEM((3,) + mat, BF16),
        pltpu.VMEM((half - 1, 3) + mat, BF16),
        pltpu.VMEM((3,) + mat, BF16),
        pltpu.VMEM((3,) + mat, BF16),
        pltpu.VMEM((3,) + mat, BF16),
        pltpu.VMEM((2, NY - 1, rows_k, shard), BF16),
        pltpu.VMEM((2, NY, rows_k, shard), BF16),
        pltpu.VMEM(pick, BF16),
        pltpu.VMEM(pick, BF16),
        pltpu.VMEM(pick, BF16),
        pltpu.VMEM((3, nx, chunk, hw), BF16),
        pltpu.VMEM((3, nx, chunk, hw), F32),
        pltpu.VMEM((3, nx, chunk, hw), BF16),
        pltpu.VMEM((nx - 1, 3, chunk, hw), BF16),
        pltpu.VMEM((nx - 1, 3, chunk, hw), BF16),
        pltpu.VMEM((3, NC, nx, chunk, hw), BF16),
        pltpu.VMEM((2, NY - 1, rows_k, shard), BF16),
        pltpu.VMEM((2, NY, rows_k, shard), BF16),
        pltpu.VMEM((2, half, 2, tok_n, shard), F32),
        pltpu.VMEM((2, 2, half, tok_n, shard), BF16),
        pltpu.VMEM((2, 2, half, tok_n, shard), BF16),
        dma((5,)),
        dma((2, 3, 2, half)),
        dma((2, 3, 3)),
        dma((2, 3, 3, 2, half)),
        dma((2, 2, NY - 1, half // 2)),
        dma((2, 3)),
        dma((2, 3, nx - 1)),
        dma((2, 3, nx - 1)),
        dma((2, 3, nx)),
        dma((2, 2, NY - 1)),
        dma((2, 2, 2, half)),
    ]
    out = pl.pallas_call(
        functools.partial(kernel, nz, nx, cap),
        name="expert_step",
        out_shape=(
            jax.ShapeDtypeStruct((tok_n, shard), BF16),
            jax.ShapeDtypeStruct((tok_n, shard), BF16),
            jax.ShapeDtypeStruct(mat, F32),
            jax.ShapeDtypeStruct(mat, BF16),
            jax.ShapeDtypeStruct(mat, BF16),
            jax.ShapeDtypeStruct(mat, BF16),
        ),
        in_specs=[smem, smem, vmem, vmem] + [anywhere] * 5,
        out_specs=(vmem,) * 6,
        scratch_shapes=scratch,
        compiler_params=pltpu.CompilerParams(
            collective_id=0, has_side_effects=True, vmem_limit_bytes=66 * 1000 * 1000
        ),
    )(
        placement,
        swap_flags,
        expert_ids.T,
        route_weight.T,
        tokens,
        cotangent,
        params[0],
        first_moment[0],
        second_moment[0],
    )
    mixed, input_grad, grad, *held = out
    tile = pl.BlockSpec((1, shard // ADAM_CUT, hw), lambda i: (i // ADAM_CUT, i % ADAM_CUT, 0))
    whole = pl.BlockSpec((tok_n, shard), lambda i: (0, 0))
    rows_shape = jax.ShapeDtypeStruct((tok_n, shard), BF16)
    *updated, mixed, input_grad = pl.pallas_call(
        adam,
        name="adam",
        grid=(3 * ADAM_CUT,),
        in_specs=[tile] * 4 + [whole] * 2,
        out_specs=[tile] * 3 + [whole] * 2,
        out_shape=[jax.ShapeDtypeStruct(mat, BF16)] * 3 + [rows_shape] * 2,
    )(grad, *held, mixed, input_grad)
    return (mixed, input_grad, *(a[None] for a in updated))


def solution(mesh):
    wide = P("ep", None, "os", None)
    placed = (P("ep", "os"), P("ep", "os"), P("ep", None), P("ep", None), P(), P(), wide, wide, wide)
    return jax.shard_map(
        on_device,
        mesh=mesh,
        in_specs=placed,
        out_specs=(P("ep", "os"), P("ep", "os"), wide, wide, wide),
        check_vma=False,
    )
```

```python
import functools

import jax
import jax.numpy as jnp
from jax import lax
from jax.experimental import pallas as pl
from jax.experimental.pallas import tpu as pltpu
from jax.sharding import PartitionSpec as P

MESH = pl.DeviceIdType.MESH
F32 = jnp.float32
BF16 = jnp.bfloat16

beta_first = 0.9
beta_second = 0.999
learn_rate = 0.01
adam_eps = 1e-08
adam_count = 10.0

RELAY = (4, 2, 8, 3, 8, 3, 5, 2)
NY = 4
NC = 2


def dot(a, b):
    return jnp.dot(a, b, preferred_element_type=F32)


def dot_nt(a, b):
    return lax.dot_general(a, b, (((1,), (1,)), ((), ())), preferred_element_type=F32)


def dot_tn(a, b):
    return lax.dot_general(a, b, (((0,), (0,)), ((), ())), preferred_element_type=F32)


def kernel(
    nz,
    nx,
    cap,
    place,
    flags,
    ids,
    rw,
    tok,
    cot,
    par,
    mom1,
    mom2,
    mixed,
    igrad,
    new_p,
    new_m,
    new_v,
    grads,
    scale_p,
    held_p,
    tc,
    mt,
    sb,
    hop,
    yb,
    zs,
    zr,
    sx,
    rx,
    p01,
    phi,
    plo,
    psnd,
    own,
    crecv,
    xs,
    xr,
    hh,
    yo,
    yr,
    prt,
    rss,
    rsr,
    s_loc,
    s_ag,
    s_y,
    s_z,
    s_yx,
    s_c,
    s_x,
    s_h,
    s_hc,
    s_yo,
    s_rs,
):
    ep = lax.axis_index("ep")
    osi = lax.axis_index("os")
    z, y = lax.div(ep, NY), lax.rem(ep, NY)
    x, c = lax.div(osi, NC), lax.rem(osi, NC)
    half = nz // 2
    rows_k = nz * cap
    chunk = NY * rows_k // (NC * nx)
    tok_n = tok.shape[0]
    started = []

    def dev(dz=0, dy=0, dx=0, other=False):
        e = lax.rem(z + dz + nz, nz) * NY + lax.rem(y + dy + NY, NY)
        o = lax.rem(x + dx + nx, nx) * NC + ((1 - c) if other else c)
        return (e, o)

    flip = 1 - 2 * lax.rem(y, 2)
    pair_y = (z * NY + y + flip, osi)

    def send(src, dst, sem, idx, to):
        cp = pltpu.make_async_remote_copy(
            src_ref=src,
            dst_ref=dst,
            send_sem=sem.at[(0,) + idx],
            recv_sem=sem.at[(1,) + idx],
            device_id=to,
            device_id_type=MESH,
        )
        cp.start()
        started.append(cp)
        return cp

    loc = [
        pltpu.make_async_copy(tok, tc.at[half - 1, 1, 0], s_loc.at[0]),
        pltpu.make_async_copy(cot, tc.at[half - 1, 1, 1], s_loc.at[1]),
    ]
    state = (par, mom1, mom2)
    loc += [pltpu.make_async_copy(state[a], sb.at[a], s_loc.at[2 + a]) for a in range(3)]
    for cp in loc:
        cp.start()
    mt[half - 1, 1, 0:8] = ids[...].astype(F32)
    mt[half - 1, 1, 8:16] = rw[...]

    peers = [dev(dz=1), dev(dz=-1)]
    peers += [dev(dy=k) for k in range(1, NY)]
    peers += [dev(dx=m) for m in range(1, nx)]
    peers += [dev(other=True)]
    barrier = pltpu.get_barrier_semaphore()
    for d in peers:
        pl.semaphore_signal(barrier, inc=1, device_id=d, device_id_type=MESH)
    pl.semaphore_wait(barrier, len(peers))
    for cp in loc[:3]:
        cp.wait()

    ag = {}

    def ag_send(s, d, part):
        src = (half - 1, 1) if s == 0 else (s - 1, d)
        ref, tail = (tc, (part,)) if part < 2 else (mt, ())
        ag[s, d, part] = send(
            ref.at[src + tail], ref.at[(s, d) + tail], s_ag, (part, d, s), dev(dz=1 if d == 0 else -1)
        )

    parts = (0, 2, 1)
    for part in parts:
        for d in range(2):
            ag_send(0, d, part)
    ycp = {(0, m): send(sb.at[0, m], yb.at[0, m], s_y, (0, m), pair_y) for m in range(3)}
    for a in (2, 1):
        loc[2 + a].wait()
        for m in range(3):
            ycp[a, m] = send(sb.at[a, m], yb.at[a, m], s_y, (a, m), pair_y)

    def held(i, iy):
        f1 = flags[1, i] == 1
        zi = lax.rem(i + half * NY, nz * NY)
        ziy = lax.rem(iy + half * NY, nz * NY)
        stay = jnp.where(flags[0, i] == 1, place[zi], place[i])
        move = jnp.where(flags[0, iy] == 1, place[ziy], place[iy])
        return jnp.where(f1, move, stay)

    experts = []
    for k in range(NY):
        yk = lax.rem(y + k, NY)
        i = z * NY + yk
        experts.append(held(i, i + 1 - 2 * lax.rem(yk, 2)).astype(F32))
    i_y = z * NY + y + flip
    i_z = lax.rem(ep + half * NY, nz * NY)
    f1_own = flags[1, ep] == 1
    f1_far = flags[1, i_z] == 1
    from_far = jnp.where(f1_own, flags[0, i_y], flags[0, ep]) == 1

    tri = (
        lax.broadcasted_iota(jnp.int32, (tok_n, tok_n), 0)
        < lax.broadcasted_iota(jnp.int32, (tok_n, tok_n), 1)
    ).astype(F32).astype(BF16)
    slots = lax.broadcasted_iota(jnp.int32, (cap, tok_n), 0).astype(F32)
    nothing = jnp.zeros((cap, tok_n), F32)

    zcp = {}
    cut = par.shape[1] // 2

    def z_hop(a, m, h):
        if h == 0:
            ycp[a, m].wait_recv()
            zs[a, m] = jnp.where(f1_far, yb[a, m], sb[a, m])
        for d in range(2):
            piece = (a, m, pl.ds(d * cut, cut))
            if h:
                zcp[a, m, d, h - 1].wait_recv()
            src = zs.at[piece] if h == 0 else hop.at[(h - 1,) + piece]
            dst = zr.at[piece] if h == half - 1 else hop.at[(h,) + piece]
            zcp[a, m, d, h] = send(src, dst, s_z, (a, m, d, h), dev(dz=1 if d == 0 else -1))

    def z_wait(a, m):
        for d in range(2):
            zcp[a, m, d, half - 1].wait_recv()

    def select(a, m):
        return jnp.where(from_far, zr[a, m], jnp.where(f1_own, yb[a, m], sb[a, m]))

    queue = [(a, m, h) for a in (2, 1) for h in range(half) for m in range(3)]

    def relay(count):
        for _ in range(min(count, len(queue))):
            z_hop(*queue.pop(0))

    def route(s):
        hits, weights = [], []
        for k in range(NY):
            for b in range(2):
                hit = jnp.where(mt[s, b, 0:8] == experts[k], 1.0, 0.0)
                hits.append(jnp.sum(hit, axis=0, keepdims=True))
                weights.append(jnp.sum(hit * mt[s, b, 8:16], axis=0, keepdims=True))
        mask = jnp.concatenate(hits, axis=0)
        slot = dot(mask.astype(BF16), tri)
        pick, pick_w = [], []
        for k in range(NY):
            for b in range(2):
                r = 2 * k + b
                keep = mask[r : r + 1] > 0.5
                one = jnp.where((slots == slot[r : r + 1]) & keep, 1.0, 0.0)
                w = one * weights[r]
                pick.append(jnp.concatenate((one, nothing) if b == 0 else (nothing, one), axis=1))
                pick_w.append(jnp.concatenate((w, nothing) if b == 0 else (nothing, w), axis=1))
        ones = jnp.concatenate(pick, axis=0).astype(BF16)
        wide = jnp.concatenate(pick_w, axis=0)
        high = wide.astype(BF16)
        p01[s] = ones
        phi[s] = high
        plo[s] = (wide - high.astype(F32)).astype(BF16)
        scale = jnp.sum(wide, axis=1, keepdims=True)
        t_in = jnp.concatenate((tc[s, 0, 0], tc[s, 1, 0]), axis=0)
        c_in = jnp.concatenate((tc[s, 0, 1], tc[s, 1, 1]), axis=0)
        picked = (dot(ones, t_in).astype(BF16), (scale * dot(ones, c_in)).astype(BF16))
        width = 2 * cap
        for a in range(2):
            for k in range(NY):
                part = picked[a][k * width : (k + 1) * width]
                if k == 0:
                    rx[a, 0, s * width : (s + 1) * width] = part
                else:
                    sx[a, k - 1, s * width : (s + 1) * width] = part

    rcp = []
    batch = 2
    width = 2 * cap
    for s in range(half + 1):
        for part in parts:
            for d in range(2):
                if (s, d, part) not in ag:
                    continue
                ag[s, d, part].wait_recv()
                if s + 1 < half - d:
                    ag_send(s + 1, d, part)
        if s > 0:
            for m in range(3):
                z_hop(0, m, s - 1)
        if s < half:
            route(s)
            if s % batch == batch - 1:
                b = s // batch
                piece = pl.ds(b * batch * width, batch * width)
                for a in range(2):
                    for k in range(1, NY):
                        rcp.append(
                            send(sx.at[a, k - 1, piece], rx.at[a, k, piece], s_yx, (a, k - 1, b), dev(dy=k))
                        )
    relay(RELAY[0])
    for cp in rcp:
        cp.wait_recv()
    for m in range(3):
        z_wait(0, m)
        held_p[m] = select(0, m)

    per = rows_k // chunk
    base_o, base_c = (1 - c) * (NY // NC), c * (NY // NC)
    ccp = []
    for arr in range(3):
        which = 0 if arr < 2 else 1
        for xi in range(nx):
            rows = rx[which, base_o + xi // per, (xi % per) * chunk : (xi % per + 1) * chunk]
            psnd[arr, xi] = dot(rows, held_p[arr]).astype(BF16)
        ccp.append(send(psnd.at[arr], crecv.at[arr], s_c, (arr,), dev(other=True)))
    relay(RELAY[1])
    for arr in range(3):
        which = 0 if arr < 2 else 1
        for xi in range(nx):
            rows = rx[which, base_c + xi // per, (xi % per) * chunk : (xi % per + 1) * chunk]
            own[arr, xi] = dot(rows, held_p[arr])
    xcp = {}
    sums = []
    for arr in range(3):
        ccp[arr].wait_recv()
        for m in range(1, nx):
            xi = lax.rem(x + m, nx)
            xs[m - 1, arr] = (own[arr, xi] + crecv[arr, xi].astype(F32)).astype(BF16)
            xcp[arr, m] = send(xs.at[m - 1, arr], xr.at[m - 1, arr], s_x, (arr, m - 1), dev(dx=m))

    relay(RELAY[2])

    def total(arr):
        acc = own[arr, x] + crecv[arr, x].astype(F32)
        for m in range(1, nx):
            xcp[arr, m].wait_recv()
            acc = acc + xr[m - 1, arr].astype(F32)
        return acc

    hcp = {}

    def spread(a):
        for m in range(1, nx):
            hcp[a, m] = send(hh.at[a, c, x], hh.at[a, c, x], s_h, (a, m - 1), dev(dx=m))
        hcp[a, 0] = send(hh.at[a, c, x], hh.at[a, c, x], s_hc, (a, 0), dev(other=True))

    own[0, x] = total(0)
    own[1, x] = total(1)
    gate, up = own[0, x], own[1, x]
    hh[0, c, x] = (gate * jax.nn.sigmoid(gate) * up).astype(BF16)
    spread(0)
    relay(RELAY[3])
    own[2, x] = total(2)
    gate, up, back = own[0, x], own[1, x], own[2, x]
    sigma = jax.nn.sigmoid(gate)
    hh[1, c, x] = (back * up * sigma * (1.0 + gate * (1.0 - sigma))).astype(BF16)
    hh[2, c, x] = (back * (gate * sigma)).astype(BF16)
    spread(1)
    spread(2)

    relay(RELAY[4])
    fcp = {}

    def forward(a):
        for m in range(1, nx):
            hcp[a, m].wait_recv()
            xi = lax.rem(x - m + nx, nx)
            fcp[a, m] = send(hh.at[a, c, xi], hh.at[a, c, xi], s_hc, (a, m), dev(other=True))

    def arrived(a):
        hcp[a, 0].wait_recv()
        for m in range(1, nx):
            fcp[a, m].wait_recv()

    bcp = {}

    def part(a, k):
        return hh[a, k // (NY // NC), (k % (NY // NC)) * per : (k % (NY // NC) + 1) * per].reshape(rows_k, -1)

    def give_back(a, k, value):
        if k == 0:
            yr[a, 0] = value
        else:
            yo[a, k - 1] = value
            bcp[a, k] = send(yo.at[a, k - 1], yr.at[a, k], s_yo, (a, k - 1), dev(dy=-k))

    forward(0)
    arrived(0)
    for k in (2, 1, 3, 0):
        give_back(0, k, dot_nt(part(0, k), held_p[2]).astype(BF16))
    relay(RELAY[5])
    forward(1)
    forward(2)
    arrived(1)
    arrived(2)
    for k in (2, 1, 3, 0):
        value = dot_nt(part(1, k), held_p[0]) + dot_nt(part(2, k), held_p[1])
        give_back(1, k, value.astype(BF16))

    for which, a, out in ((0, 1, 0), (0, 2, 1), (1, 0, 2)):
        for k in range(NY):
            term = dot_tn(rx[which, k], part(a, k))
            grads[out] = term if k == 0 else grads[out] + term

    relay(RELAY[6])
    def combine(a):
        for k in range(1, NY):
            bcp[a, k].wait_recv()
        for s in range(half - 1, -1, -1):
            rows = jnp.concatenate([yr[a, k, s * width : (s + 1) * width] for k in range(NY)], axis=0)
            if a == 0:
                value = dot_tn(phi[s], rows) + dot_tn(plo[s], rows)
            else:
                value = dot_tn(p01[s], rows)
            prt[a, s, 0] = value[:tok_n]
            prt[a, s, 1] = value[tok_n:]

    combine(0)
    combine(1)
    def second_moment(k):
        z_wait(2, k)
        grad = grads[k]
        v = beta_second * select(2, k).astype(F32) + (1.0 - beta_second) * grad * grad
        new_v[k] = v.astype(BF16)
        root = jnp.sqrt(v * (1.0 / (1.0 - beta_second**adam_count)))
        scale_p[k] = (learn_rate / (1.0 - beta_first**adam_count)) / (root + adam_eps)

    def first_moment(k):
        z_wait(1, k)
        m = beta_first * select(1, k).astype(F32) + (1.0 - beta_first) * grads[k]
        new_m[k] = m.astype(BF16)
        new_p[k] = (held_p[k].astype(F32) - m * scale_p[k]).astype(BF16)

    last = {}
    for t in range(half):
        for a in range(2):
            for d in range(2):
                steps = half - d
                if t >= steps:
                    continue
                value = prt[a, steps - 1 - t, d]
                if t:
                    last[a, d].wait_recv()
                    value = value + rsr[a, d, t - 1].astype(F32)
                rss[a, d, t] = value.astype(BF16)
                last[a, d] = send(
                    rss.at[a, d, t], rsr.at[a, d, t], s_rs, (a, d, t), dev(dz=-1 if d == 0 else 1)
                )
        relay(RELAY[7])
        if t < 3:
            second_moment(t)
    relay(len(queue))
    first_moment(0)
    first_moment(1)
    for a, out in ((0, mixed), (1, igrad)):
        value = prt[a, half - 1, 1]
        for d in range(2):
            last[a, d].wait_recv()
            value = value + rsr[a, d, half - d - 1].astype(F32)
        out[...] = value.astype(BF16)

    first_moment(2)

    for cp in started:
        cp.wait_send()


def hand_over(*refs):
    n = (len(refs) - 1) // 3
    src, dst, held, sem = refs[:n], refs[n : 2 * n], refs[2 * n : 3 * n], refs[-1]
    into = [pltpu.make_async_copy(src[i], held[i], sem.at[0, i]) for i in range(n)]
    out = [pltpu.make_async_copy(held[i], dst[i], sem.at[1, i]) for i in range(n)]
    for cp in into:
        cp.start()
    for i in range(n):
        into[i].wait()
        out[i].start()
    for cp in out:
        cp.wait()


def on_device(tokens, cotangent, expert_ids, route_weight, placement, swap_flags, params, first_moment, second_moment):
    nz = lax.axis_size("ep") // NY
    nx = lax.axis_size("os") // NC
    tok_n, shard = tokens.shape
    top = expert_ids.shape[1]
    _, _, _, hw = params.shape
    cap = max(2, 3 * tok_n * top // (2 * lax.axis_size("ep")))
    half = nz // 2
    rows_k = nz * cap
    chunk = NY * rows_k // (NC * nx)
    vmem = pl.BlockSpec(memory_space=pltpu.VMEM)
    smem = pl.BlockSpec(memory_space=pltpu.SMEM)
    anywhere = pl.BlockSpec(memory_space=pl.ANY)
    mat = (3, shard, hw)
    dma = pltpu.SemaphoreType.DMA
    pick = (half, NY * 2 * cap, 2 * tok_n)
    scratch = [
        pltpu.VMEM(mat, F32),
        pltpu.VMEM(mat, F32),
        pltpu.VMEM(mat, BF16),
        pltpu.VMEM((half, 2, 2, tok_n, shard), BF16),
        pltpu.VMEM((half, 2, 2 * top, tok_n), F32),
        pltpu.VMEM((3,) + mat, BF16),
        pltpu.VMEM((half - 1, 3) + mat, BF16),
        pltpu.VMEM((3,) + mat, BF16),
        pltpu.VMEM((3,) + mat, BF16),
        pltpu.VMEM((3,) + mat, BF16),
        pltpu.VMEM((2, NY - 1, rows_k, shard), BF16),
        pltpu.VMEM((2, NY, rows_k, shard), BF16),
        pltpu.VMEM(pick, BF16),
        pltpu.VMEM(pick, BF16),
        pltpu.VMEM(pick, BF16),
        pltpu.VMEM((3, nx, chunk, hw), BF16),
        pltpu.VMEM((3, nx, chunk, hw), F32),
        pltpu.VMEM((3, nx, chunk, hw), BF16),
        pltpu.VMEM((nx - 1, 3, chunk, hw), BF16),
        pltpu.VMEM((nx - 1, 3, chunk, hw), BF16),
        pltpu.VMEM((3, NC, nx, chunk, hw), BF16),
        pltpu.VMEM((2, NY - 1, rows_k, shard), BF16),
        pltpu.VMEM((2, NY, rows_k, shard), BF16),
        pltpu.VMEM((2, half, 2, tok_n, shard), F32),
        pltpu.VMEM((2, 2, half, tok_n, shard), BF16),
        pltpu.VMEM((2, 2, half, tok_n, shard), BF16),
        dma((5,)),
        dma((2, 3, 2, half)),
        dma((2, 3, 3)),
        dma((2, 3, 3, 2, half)),
        dma((2, 2, NY - 1, half // 2)),
        dma((2, 3)),
        dma((2, 3, nx - 1)),
        dma((2, 3, nx - 1)),
        dma((2, 3, nx)),
        dma((2, 2, NY - 1)),
        dma((2, 2, 2, half)),
    ]
    out = pl.pallas_call(
        functools.partial(kernel, nz, nx, cap),
        name="expert_step",
        out_shape=(
            jax.ShapeDtypeStruct((tok_n, shard), BF16),
            jax.ShapeDtypeStruct((tok_n, shard), BF16),
            jax.ShapeDtypeStruct(mat, BF16),
            jax.ShapeDtypeStruct(mat, BF16),
            jax.ShapeDtypeStruct(mat, BF16),
        ),
        in_specs=[smem, smem, vmem, vmem] + [anywhere] * 5,
        out_specs=(vmem,) * 5,
        scratch_shapes=scratch,
        compiler_params=pltpu.CompilerParams(
            collective_id=0, has_side_effects=True, vmem_limit_bytes=66 * 1000 * 1000
        ),
    )(
        placement,
        swap_flags,
        expert_ids.T,
        route_weight.T,
        tokens,
        cotangent,
        params[0],
        first_moment[0],
        second_moment[0],
    )
    shapes = [jax.ShapeDtypeStruct(a.shape, BF16) for a in out]
    mixed, input_grad, *updated = pl.pallas_call(
        hand_over,
        name="hand_over",
        in_specs=[anywhere] * 5,
        out_specs=[anywhere] * 5,
        out_shape=shapes,
        scratch_shapes=[pltpu.VMEM(a.shape, BF16) for a in shapes] + [dma((2, 5))],
    )(*out)
    return (mixed, input_grad, *(a[None] for a in updated))


def solution(mesh):
    wide = P("ep", None, "os", None)
    placed = (P("ep", "os"), P("ep", "os"), P("ep", None), P("ep", None), P(), P(), wide, wide, wide)
    return jax.shard_map(
        on_device,
        mesh=mesh,
        in_specs=placed,
        out_specs=(P("ep", "os"), P("ep", "os"), wide, wide, wide),
        check_vma=False,
    )
```

```python
import functools

import jax
import jax.numpy as jnp
from jax import lax
from jax.experimental import pallas as pl
from jax.experimental.pallas import tpu as pltpu
from jax.sharding import PartitionSpec as P

MESH = pl.DeviceIdType.MESH
F32 = jnp.float32
BF16 = jnp.bfloat16

beta_first = 0.9
beta_second = 0.999
learn_rate = 0.01
adam_eps = 1e-08
adam_count = 10.0

RELAY = (4, 2, 8, 3, 8, 3, 5, 2)
NY = 4
NC = 2


def dot(a, b):
    return jnp.dot(a, b, preferred_element_type=F32)


def dot_nt(a, b):
    return lax.dot_general(a, b, (((1,), (1,)), ((), ())), preferred_element_type=F32)


def dot_tn(a, b):
    return lax.dot_general(a, b, (((0,), (0,)), ((), ())), preferred_element_type=F32)


def kernel(
    nz,
    nx,
    cap,
    place,
    flags,
    ids,
    rw,
    tok,
    cot,
    par,
    mom1,
    mom2,
    mixed,
    igrad,
    out_p,
    out_m,
    out_v,
    new_p,
    new_m,
    new_v,
    s_out,
    grads,
    scale_p,
    held_p,
    tc,
    mt,
    sb,
    hop,
    yb,
    zs,
    zr,
    sx,
    rx,
    p01,
    phi,
    plo,
    psnd,
    own,
    crecv,
    xs,
    xr,
    hh,
    yo,
    yr,
    prt,
    rss,
    rsr,
    s_loc,
    s_ag,
    s_y,
    s_z,
    s_yx,
    s_c,
    s_x,
    s_h,
    s_hc,
    s_yo,
    s_rs,
):
    ep = lax.axis_index("ep")
    osi = lax.axis_index("os")
    z, y = lax.div(ep, NY), lax.rem(ep, NY)
    x, c = lax.div(osi, NC), lax.rem(osi, NC)
    half = nz // 2
    rows_k = nz * cap
    chunk = NY * rows_k // (NC * nx)
    tok_n = tok.shape[0]
    started = []

    def dev(dz=0, dy=0, dx=0, other=False):
        e = lax.rem(z + dz + nz, nz) * NY + lax.rem(y + dy + NY, NY)
        o = lax.rem(x + dx + nx, nx) * NC + ((1 - c) if other else c)
        return (e, o)

    flip = 1 - 2 * lax.rem(y, 2)
    pair_y = (z * NY + y + flip, osi)

    def send(src, dst, sem, idx, to):
        cp = pltpu.make_async_remote_copy(
            src_ref=src,
            dst_ref=dst,
            send_sem=sem.at[(0,) + idx],
            recv_sem=sem.at[(1,) + idx],
            device_id=to,
            device_id_type=MESH,
        )
        cp.start()
        started.append(cp)
        return cp

    loc = [
        pltpu.make_async_copy(tok, tc.at[half - 1, 1, 0], s_loc.at[0]),
        pltpu.make_async_copy(cot, tc.at[half - 1, 1, 1], s_loc.at[1]),
    ]
    state = (par, mom1, mom2)
    loc += [pltpu.make_async_copy(state[a], sb.at[a], s_loc.at[2 + a]) for a in range(3)]
    for cp in loc:
        cp.start()
    mt[half - 1, 1, 0:8] = ids[...].astype(F32)
    mt[half - 1, 1, 8:16] = rw[...]

    peers = [dev(dz=1), dev(dz=-1)]
    peers += [dev(dy=k) for k in range(1, NY)]
    peers += [dev(dx=m) for m in range(1, nx)]
    peers += [dev(other=True)]
    barrier = pltpu.get_barrier_semaphore()
    for d in peers:
        pl.semaphore_signal(barrier, inc=1, device_id=d, device_id_type=MESH)
    pl.semaphore_wait(barrier, len(peers))
    for cp in loc[:3]:
        cp.wait()

    ag = {}

    def ag_send(s, d, part):
        src = (half - 1, 1) if s == 0 else (s - 1, d)
        ref, tail = (tc, (part,)) if part < 2 else (mt, ())
        ag[s, d, part] = send(
            ref.at[src + tail], ref.at[(s, d) + tail], s_ag, (part, d, s), dev(dz=1 if d == 0 else -1)
        )

    parts = (0, 2, 1)
    for part in parts:
        for d in range(2):
            ag_send(0, d, part)
    ycp = {(0, m): send(sb.at[0, m], yb.at[0, m], s_y, (0, m), pair_y) for m in range(3)}
    for a in (2, 1):
        loc[2 + a].wait()
        for m in range(3):
            ycp[a, m] = send(sb.at[a, m], yb.at[a, m], s_y, (a, m), pair_y)

    def held(i, iy):
        f1 = flags[1, i] == 1
        zi = lax.rem(i + half * NY, nz * NY)
        ziy = lax.rem(iy + half * NY, nz * NY)
        stay = jnp.where(flags[0, i] == 1, place[zi], place[i])
        move = jnp.where(flags[0, iy] == 1, place[ziy], place[iy])
        return jnp.where(f1, move, stay)

    experts = []
    for k in range(NY):
        yk = lax.rem(y + k, NY)
        i = z * NY + yk
        experts.append(held(i, i + 1 - 2 * lax.rem(yk, 2)).astype(F32))
    i_y = z * NY + y + flip
    i_z = lax.rem(ep + half * NY, nz * NY)
    f1_own = flags[1, ep] == 1
    f1_far = flags[1, i_z] == 1
    from_far = jnp.where(f1_own, flags[0, i_y], flags[0, ep]) == 1

    tri = (
        lax.broadcasted_iota(jnp.int32, (tok_n, tok_n), 0)
        < lax.broadcasted_iota(jnp.int32, (tok_n, tok_n), 1)
    ).astype(F32).astype(BF16)
    slots = lax.broadcasted_iota(jnp.int32, (cap, tok_n), 0).astype(F32)
    nothing = jnp.zeros((cap, tok_n), F32)

    zcp = {}
    cut = par.shape[1] // 2

    def z_hop(a, m, h):
        if h == 0:
            ycp[a, m].wait_recv()
            zs[a, m] = jnp.where(f1_far, yb[a, m], sb[a, m])
        for d in range(2):
            piece = (a, m, pl.ds(d * cut, cut))
            if h:
                zcp[a, m, d, h - 1].wait_recv()
            src = zs.at[piece] if h == 0 else hop.at[(h - 1,) + piece]
            dst = zr.at[piece] if h == half - 1 else hop.at[(h,) + piece]
            zcp[a, m, d, h] = send(src, dst, s_z, (a, m, d, h), dev(dz=1 if d == 0 else -1))

    def z_wait(a, m):
        for d in range(2):
            zcp[a, m, d, half - 1].wait_recv()

    def select(a, m):
        return jnp.where(from_far, zr[a, m], jnp.where(f1_own, yb[a, m], sb[a, m]))

    queue = [(a, m, h) for a in (2, 1) for h in range(half) for m in range(3)]

    def relay(count):
        for _ in range(min(count, len(queue))):
            z_hop(*queue.pop(0))

    def route(s):
        hits, weights = [], []
        for k in range(NY):
            for b in range(2):
                hit = jnp.where(mt[s, b, 0:8] == experts[k], 1.0, 0.0)
                hits.append(jnp.sum(hit, axis=0, keepdims=True))
                weights.append(jnp.sum(hit * mt[s, b, 8:16], axis=0, keepdims=True))
        mask = jnp.concatenate(hits, axis=0)
        slot = dot(mask.astype(BF16), tri)
        pick, pick_w = [], []
        for k in range(NY):
            for b in range(2):
                r = 2 * k + b
                keep = mask[r : r + 1] > 0.5
                one = jnp.where((slots == slot[r : r + 1]) & keep, 1.0, 0.0)
                w = one * weights[r]
                pick.append(jnp.concatenate((one, nothing) if b == 0 else (nothing, one), axis=1))
                pick_w.append(jnp.concatenate((w, nothing) if b == 0 else (nothing, w), axis=1))
        ones = jnp.concatenate(pick, axis=0).astype(BF16)
        wide = jnp.concatenate(pick_w, axis=0)
        high = wide.astype(BF16)
        p01[s] = ones
        phi[s] = high
        plo[s] = (wide - high.astype(F32)).astype(BF16)
        scale = jnp.sum(wide, axis=1, keepdims=True)
        t_in = jnp.concatenate((tc[s, 0, 0], tc[s, 1, 0]), axis=0)
        c_in = jnp.concatenate((tc[s, 0, 1], tc[s, 1, 1]), axis=0)
        picked = (dot(ones, t_in).astype(BF16), (scale * dot(ones, c_in)).astype(BF16))
        width = 2 * cap
        for a in range(2):
            for k in range(NY):
                part = picked[a][k * width : (k + 1) * width]
                if k == 0:
                    rx[a, 0, s * width : (s + 1) * width] = part
                else:
                    sx[a, k - 1, s * width : (s + 1) * width] = part

    rcp = []
    batch = 2
    width = 2 * cap
    for s in range(half + 1):
        for part in parts:
            for d in range(2):
                if (s, d, part) not in ag:
                    continue
                ag[s, d, part].wait_recv()
                if s + 1 < half - d:
                    ag_send(s + 1, d, part)
        if s > 0:
            for m in range(3):
                z_hop(0, m, s - 1)
        if s < half:
            route(s)
            if s % batch == batch - 1:
                b = s // batch
                piece = pl.ds(b * batch * width, batch * width)
                for a in range(2):
                    for k in range(1, NY):
                        rcp.append(
                            send(sx.at[a, k - 1, piece], rx.at[a, k, piece], s_yx, (a, k - 1, b), dev(dy=k))
                        )
    relay(RELAY[0])
    for cp in rcp:
        cp.wait_recv()
    for m in range(3):
        z_wait(0, m)
        held_p[m] = select(0, m)

    per = rows_k // chunk
    base_o, base_c = (1 - c) * (NY // NC), c * (NY // NC)
    ccp = []
    for arr in range(3):
        which = 0 if arr < 2 else 1
        for xi in range(nx):
            rows = rx[which, base_o + xi // per, (xi % per) * chunk : (xi % per + 1) * chunk]
            psnd[arr, xi] = dot(rows, held_p[arr]).astype(BF16)
        ccp.append(send(psnd.at[arr], crecv.at[arr], s_c, (arr,), dev(other=True)))
    relay(RELAY[1])
    for arr in range(3):
        which = 0 if arr < 2 else 1
        for xi in range(nx):
            rows = rx[which, base_c + xi // per, (xi % per) * chunk : (xi % per + 1) * chunk]
            own[arr, xi] = dot(rows, held_p[arr])
    xcp = {}
    sums = []
    for arr in range(3):
        ccp[arr].wait_recv()
        for m in range(1, nx):
            xi = lax.rem(x + m, nx)
            xs[m - 1, arr] = (own[arr, xi] + crecv[arr, xi].astype(F32)).astype(BF16)
            xcp[arr, m] = send(xs.at[m - 1, arr], xr.at[m - 1, arr], s_x, (arr, m - 1), dev(dx=m))

    relay(RELAY[2])

    def total(arr):
        acc = own[arr, x] + crecv[arr, x].astype(F32)
        for m in range(1, nx):
            xcp[arr, m].wait_recv()
            acc = acc + xr[m - 1, arr].astype(F32)
        return acc

    hcp = {}

    def spread(a):
        for m in range(1, nx):
            hcp[a, m] = send(hh.at[a, c, x], hh.at[a, c, x], s_h, (a, m - 1), dev(dx=m))
        hcp[a, 0] = send(hh.at[a, c, x], hh.at[a, c, x], s_hc, (a, 0), dev(other=True))

    own[0, x] = total(0)
    own[1, x] = total(1)
    gate, up = own[0, x], own[1, x]
    hh[0, c, x] = (gate * jax.nn.sigmoid(gate) * up).astype(BF16)
    spread(0)
    relay(RELAY[3])
    own[2, x] = total(2)
    gate, up, back = own[0, x], own[1, x], own[2, x]
    sigma = jax.nn.sigmoid(gate)
    hh[1, c, x] = (back * up * sigma * (1.0 + gate * (1.0 - sigma))).astype(BF16)
    hh[2, c, x] = (back * (gate * sigma)).astype(BF16)
    spread(1)
    spread(2)

    relay(RELAY[4])
    fcp = {}

    def forward(a):
        for m in range(1, nx):
            hcp[a, m].wait_recv()
            xi = lax.rem(x - m + nx, nx)
            fcp[a, m] = send(hh.at[a, c, xi], hh.at[a, c, xi], s_hc, (a, m), dev(other=True))

    def arrived(a):
        hcp[a, 0].wait_recv()
        for m in range(1, nx):
            fcp[a, m].wait_recv()

    bcp = {}

    def part(a, k):
        return hh[a, k // (NY // NC), (k % (NY // NC)) * per : (k % (NY // NC) + 1) * per].reshape(rows_k, -1)

    def give_back(a, k, value):
        if k == 0:
            yr[a, 0] = value
        else:
            yo[a, k - 1] = value
            bcp[a, k] = send(yo.at[a, k - 1], yr.at[a, k], s_yo, (a, k - 1), dev(dy=-k))

    forward(0)
    arrived(0)
    for k in (2, 1, 3, 0):
        give_back(0, k, dot_nt(part(0, k), held_p[2]).astype(BF16))
    relay(RELAY[5])
    forward(1)
    forward(2)
    arrived(1)
    arrived(2)
    for k in (2, 1, 3, 0):
        value = dot_nt(part(1, k), held_p[0]) + dot_nt(part(2, k), held_p[1])
        give_back(1, k, value.astype(BF16))

    for which, a, out in ((0, 1, 0), (0, 2, 1), (1, 0, 2)):
        for k in range(NY):
            term = dot_tn(rx[which, k], part(a, k))
            grads[out] = term if k == 0 else grads[out] + term

    relay(RELAY[6])
    def combine(a):
        for k in range(1, NY):
            bcp[a, k].wait_recv()
        for s in range(half - 1, -1, -1):
            rows = jnp.concatenate([yr[a, k, s * width : (s + 1) * width] for k in range(NY)], axis=0)
            if a == 0:
                value = dot_tn(phi[s], rows) + dot_tn(plo[s], rows)
            else:
                value = dot_tn(p01[s], rows)
            prt[a, s, 0] = value[:tok_n]
            prt[a, s, 1] = value[tok_n:]

    combine(0)
    combine(1)
    written = []

    def write(n, k):
        src, dst = ((new_p, out_p), (new_m, out_m), (new_v, out_v))[n]
        written.append(pltpu.make_async_copy(src.at[k], dst.at[k], s_out.at[n, k]))
        written[-1].start()

    def second_moment(k):
        z_wait(2, k)
        grad = grads[k]
        v = beta_second * select(2, k).astype(F32) + (1.0 - beta_second) * grad * grad
        new_v[k] = v.astype(BF16)
        write(2, k)
        root = jnp.sqrt(v * (1.0 / (1.0 - beta_second**adam_count)))
        scale_p[k] = (learn_rate / (1.0 - beta_first**adam_count)) / (root + adam_eps)

    def first_moment(k):
        z_wait(1, k)
        m = beta_first * select(1, k).astype(F32) + (1.0 - beta_first) * grads[k]
        new_m[k] = m.astype(BF16)
        new_p[k] = (held_p[k].astype(F32) - m * scale_p[k]).astype(BF16)
        write(1, k)
        write(0, k)

    last = {}
    for t in range(half):
        for a in range(2):
            for d in range(2):
                steps = half - d
                if t >= steps:
                    continue
                value = prt[a, steps - 1 - t, d]
                if t:
                    last[a, d].wait_recv()
                    value = value + rsr[a, d, t - 1].astype(F32)
                rss[a, d, t] = value.astype(BF16)
                last[a, d] = send(
                    rss.at[a, d, t], rsr.at[a, d, t], s_rs, (a, d, t), dev(dz=-1 if d == 0 else 1)
                )
        relay(RELAY[7])
        if t < 3:
            second_moment(t)
    relay(len(queue))
    first_moment(0)
    first_moment(1)
    for a, out in ((0, mixed), (1, igrad)):
        value = prt[a, half - 1, 1]
        for d in range(2):
            last[a, d].wait_recv()
            value = value + rsr[a, d, half - d - 1].astype(F32)
        out[...] = value.astype(BF16)

    first_moment(2)
    for cp in written:
        cp.wait()

    for cp in started:
        cp.wait_send()


def hand_over(*refs):
    n = (len(refs) - 1) // 3
    src, dst, held, sem = refs[:n], refs[n : 2 * n], refs[2 * n : 3 * n], refs[-1]
    into = [pltpu.make_async_copy(src[i], held[i], sem.at[0, i]) for i in range(n)]
    out = [pltpu.make_async_copy(held[i], dst[i], sem.at[1, i]) for i in range(n)]
    for cp in into:
        cp.start()
    for i in range(n):
        into[i].wait()
        out[i].start()
    for cp in out:
        cp.wait()


def on_device(tokens, cotangent, expert_ids, route_weight, placement, swap_flags, params, first_moment, second_moment):
    nz = lax.axis_size("ep") // NY
    nx = lax.axis_size("os") // NC
    tok_n, shard = tokens.shape
    top = expert_ids.shape[1]
    _, _, _, hw = params.shape
    cap = max(2, 3 * tok_n * top // (2 * lax.axis_size("ep")))
    half = nz // 2
    rows_k = nz * cap
    chunk = NY * rows_k // (NC * nx)
    vmem = pl.BlockSpec(memory_space=pltpu.VMEM)
    smem = pl.BlockSpec(memory_space=pltpu.SMEM)
    anywhere = pl.BlockSpec(memory_space=pl.ANY)
    mat = (3, shard, hw)
    dma = pltpu.SemaphoreType.DMA
    pick = (half, NY * 2 * cap, 2 * tok_n)
    scratch = [
        pltpu.VMEM(mat, BF16),
        pltpu.VMEM(mat, BF16),
        pltpu.VMEM(mat, BF16),
        dma((3, 3)),
        pltpu.VMEM(mat, F32),
        pltpu.VMEM(mat, F32),
        pltpu.VMEM(mat, BF16),
        pltpu.VMEM((half, 2, 2, tok_n, shard), BF16),
        pltpu.VMEM((half, 2, 2 * top, tok_n), F32),
        pltpu.VMEM((3,) + mat, BF16),
        pltpu.VMEM((half - 1, 3) + mat, BF16),
        pltpu.VMEM((3,) + mat, BF16),
        pltpu.VMEM((3,) + mat, BF16),
        pltpu.VMEM((3,) + mat, BF16),
        pltpu.VMEM((2, NY - 1, rows_k, shard), BF16),
        pltpu.VMEM((2, NY, rows_k, shard), BF16),
        pltpu.VMEM(pick, BF16),
        pltpu.VMEM(pick, BF16),
        pltpu.VMEM(pick, BF16),
        pltpu.VMEM((3, nx, chunk, hw), BF16),
        pltpu.VMEM((3, nx, chunk, hw), F32),
        pltpu.VMEM((3, nx, chunk, hw), BF16),
        pltpu.VMEM((nx - 1, 3, chunk, hw), BF16),
        pltpu.VMEM((nx - 1, 3, chunk, hw), BF16),
        pltpu.VMEM((3, NC, nx, chunk, hw), BF16),
        pltpu.VMEM((2, NY - 1, rows_k, shard), BF16),
        pltpu.VMEM((2, NY, rows_k, shard), BF16),
        pltpu.VMEM((2, half, 2, tok_n, shard), F32),
        pltpu.VMEM((2, 2, half, tok_n, shard), BF16),
        pltpu.VMEM((2, 2, half, tok_n, shard), BF16),
        dma((5,)),
        dma((2, 3, 2, half)),
        dma((2, 3, 3)),
        dma((2, 3, 3, 2, half)),
        dma((2, 2, NY - 1, half // 2)),
        dma((2, 3)),
        dma((2, 3, nx - 1)),
        dma((2, 3, nx - 1)),
        dma((2, 3, nx)),
        dma((2, 2, NY - 1)),
        dma((2, 2, 2, half)),
    ]
    out = pl.pallas_call(
        functools.partial(kernel, nz, nx, cap),
        name="expert_step",
        out_shape=(
            jax.ShapeDtypeStruct((tok_n, shard), BF16),
            jax.ShapeDtypeStruct((tok_n, shard), BF16),
            jax.ShapeDtypeStruct(mat, BF16),
            jax.ShapeDtypeStruct(mat, BF16),
            jax.ShapeDtypeStruct(mat, BF16),
        ),
        in_specs=[smem, smem, vmem, vmem] + [anywhere] * 5,
        out_specs=(vmem,) * 2 + (anywhere,) * 3,
        scratch_shapes=scratch,
        compiler_params=pltpu.CompilerParams(
            collective_id=0, has_side_effects=True, vmem_limit_bytes=66 * 1000 * 1000
        ),
    )(
        placement,
        swap_flags,
        expert_ids.T,
        route_weight.T,
        tokens,
        cotangent,
        params[0],
        first_moment[0],
        second_moment[0],
    )
    shapes = [jax.ShapeDtypeStruct(a.shape, BF16) for a in out]
    mixed, input_grad, *updated = pl.pallas_call(
        hand_over,
        name="hand_over",
        in_specs=[anywhere] * 5,
        out_specs=[anywhere] * 5,
        out_shape=shapes,
        scratch_shapes=[pltpu.VMEM(a.shape, BF16) for a in shapes] + [dma((2, 5))],
    )(*out)
    return (mixed, input_grad, *(a[None] for a in updated))


def solution(mesh):
    wide = P("ep", None, "os", None)
    placed = (P("ep", "os"), P("ep", "os"), P("ep", None), P("ep", None), P(), P(), wide, wide, wide)
    return jax.shard_map(
        on_device,
        mesh=mesh,
        in_specs=placed,
        out_specs=(P("ep", "os"), P("ep", "os"), wide, wide, wide),
        check_vma=False,
    )
```
